32 devices in a mesh: fsdp: 8 (over y, x, core), rep: 4 (over z).
Axes of the slice: x: 2, y: 2, z: 4, core: 2. Of those that a mesh axis runs over, the one named last changes fastest.
Arguments:
- inputs: bfloat16 [4, 1024, 4096], P('rep', 'fsdp'), may hold values from -6 to 6
- out_grad: bfloat16 [4, 1024, 512], P('rep', 'fsdp'), may hold values from -6 to 6
- weight: bfloat16 [4096, 512], P('fsdp'), may hold values from -6 to 6
- momentum: float32 [4, 512, 4096], P('rep', 'fsdp'), may hold values from -6 to 6
- band_index: int32 [128], replicated, may hold values from 0 to 511, as said below
Outputs:
- leftover: float32 [4, 512, 4096], P('rep', 'fsdp')
- new_weight: bfloat16 [4096, 512], P('fsdp')
- values: bfloat16 [4, 1024, 512], P('rep', 'fsdp')
The draws below stay inside these ranges and needn't reach their ends.
Inputs may be any that keep to these rules, and one draw needn't show every extreme that they name: `band_index`: distinct entries below 512; 0 and 511 are always among them.
All inputs are finite; a program needn't handle non-finite values.
Results may differ from the reference program's by a relative error of at most 0.0049.
Values may be sent and summed in bfloat16 or wider, within the bound.
A program may use at most 64 MiB of HBM per device.

```python
import math
import jax
import jax.numpy as jnp
from jax import lax

D = 4096
KVW = 512
GROUP = 4096
BAND = 128
LOW = 512
TOKENS = 1024
GROUPS = 512
N_REP = 4


def draw_band_index(key, part):
    middle = jax.random.permutation(jax.random.fold_in(key, 7), LOW - 2)[:BAND - 2] + 1
    ends = jnp.array([0, LOW - 1], dtype=jnp.int32)
    return jnp.concatenate([ends, middle.astype(jnp.int32)]).astype(jnp.int32)


def spiked(entries, rng, source, target, blocks, factor):
    def block_of(axis_at):
        return (jnp.arange(entries.shape[axis_at]) // (entries.shape[axis_at] // blocks)).reshape((-1,) + (1,) * (entries.ndim - 1 - axis_at))

    first = jax.random.permutation(rng, blocks)[block_of(target)]
    second = (block_of(target) + blocks // 2) % blocks
    return jnp.where((block_of(source) == first) | (block_of(source) == second), factor * entries, entries)


def shard_levels(own_key, dims, cuts, low, largest):
    loudness = 1.0
    for axis_at, parts in cuts:
        heights = jax.random.uniform(jax.random.fold_in(jax.random.fold_in(own_key, 6), axis_at), (parts,), jnp.float32, low / len(cuts), largest / len(cuts))
        loudness = loudness * jnp.repeat(jnp.exp(heights), dims[axis_at] // parts).reshape((-1,) + (1,) * (len(dims) - 1 - axis_at))
    return loudness


def normal_values(rng, extent, scale, limit, split=(), held_as=jnp.bfloat16):
    result = jax.random.normal(rng, extent, jnp.float32) * scale
    if len(split) > 0:
        result = shard_levels(rng, extent, split, -0.22, 0.18) * result
    return jnp.clip(result, min=-limit, max=limit).astype(held_as)


def bell_draw_with(stream_key, dims, spread, reach, split, heavy, held_as=jnp.bfloat16):
    drawn = spread * jax.random.normal(stream_key, dims, jnp.float32)
    if split:
        drawn = drawn * shard_levels(stream_key, dims, split, -0.22, 0.18)
    return jnp.clip(spiked(drawn, jax.random.fold_in(stream_key, 3), *heavy), -reach, reach).astype(held_as)


def setup_inputs(seed: int = 0) -> dict:
    key_list = jax.random.split(jax.random.key(seed), 6)
    inputs = bell_draw_with(key_list[0], (N_REP, TOKENS, D), 1.0, 6.0, ((0, 4), (1, 8)), (1, 2, 8, 2.0))
    out_grad = normal_values(key_list[1], (N_REP, TOKENS, KVW), 1.0, 6.0, ((0, 4), (1, 8)))
    weight = normal_values(key_list[2], (D, KVW), 1.0, 6.0, ((0, 8),))
    momentum = normal_values(key_list[3], (N_REP, GROUPS, GROUP), 1.0, 6.0, ((0, 4), (1, 8)), jnp.float32)
    band_index = draw_band_index(jax.random.fold_in(key_list[5], 71), 0)
    return dict(inputs=inputs, out_grad=out_grad, weight=weight, momentum=momentum, band_index=band_index)


MOMENTUM_DECAY = 0.9
LEARNING_RATE = 4.0

def dct_rows(band_index, length):
    positions = lax.iota(jnp.int32, length)
    freqs = band_index.astype(jnp.int32)
    phase_int = (2 * positions[None, :] + 1) * freqs[:, None] % (4 * length)
    angles = phase_int.astype(jnp.float32) * (math.pi / (2 * length))
    row_scale = jnp.where(freqs == 0, math.sqrt(1.0 / length), math.sqrt(2.0 / length)).astype(jnp.float32)
    return row_scale[:, None] * jnp.cos(angles)

def reference(inputs, out_grad, weight, momentum, band_index):
    dct_basis = dct_rows(band_index, GROUP)
    scaling = 1.0 / math.sqrt(D)
    highest = lax.Precision.HIGHEST

    def per_replica(replica_args):
        tok_inputs, upstream, old_moment = replica_args
        gradient = jnp.dot(tok_inputs.T, upstream, preferred_element_type=jnp.float32) * scaling
        moment = MOMENTUM_DECAY * old_moment + gradient.reshape(GROUPS, GROUP)
        coeffs = jnp.dot(moment, dct_basis.T, precision=highest)
        kept = moment - jnp.dot(coeffs, dct_basis, precision=highest)
        return (kept, coeffs)
    leftover, coeffs = lax.map(per_replica, (inputs, out_grad, momentum))
    shared = lax.optimization_barrier(jnp.sum(coeffs, axis=0)) / N_REP
    update_full = jnp.dot(shared, dct_basis, precision=highest).reshape(D, KVW)
    new_weight = (weight.astype(jnp.float32) - LEARNING_RATE * update_full).astype(jnp.bfloat16)

    def project(tok_inputs):
        return (jnp.dot(tok_inputs, new_weight, preferred_element_type=jnp.float32) * scaling).astype(jnp.bfloat16)
    values = lax.map(project, inputs)
    return (leftover, new_weight, values)
```

```python
import functools
import math

import jax
import jax.numpy as jnp
from jax import lax
from jax.experimental import pallas as pl
from jax.experimental.pallas import tpu as pltpu
from jax.sharding import PartitionSpec as P

MOMENTUM_DECAY = 0.9
LEARNING_RATE = 4.0


def dct_rows(band_index, length):
    positions = lax.iota(jnp.int32, length)
    phase_int = (2 * positions[None, :] + 1) * band_index[:, None] % (4 * length)
    angles = phase_int.astype(jnp.float32) * (math.pi / (2 * length))
    row_scale = jnp.where(band_index == 0, math.sqrt(1.0 / length), math.sqrt(2.0 / length)).astype(
        jnp.float32
    )
    return row_scale[:, None] * jnp.cos(angles)


def rebuild_rows(old_rows, update_rows):
    return (old_rows.astype(jnp.float32) - LEARNING_RATE * update_rows).astype(jnp.bfloat16)


def shards(inputs, out_grad, weight, momentum, band_index):
    tok_inputs = inputs[0]
    upstream = out_grad[0]
    own_rows = weight.shape[0]
    width_out = weight.shape[1]
    group_len = momentum.shape[2]
    scaling = 1.0 / math.sqrt(tok_inputs.shape[1])
    highest = lax.Precision.HIGHEST
    own_columns = lax.all_to_all(tok_inputs, "fsdp", split_axis=1, concat_axis=0, tiled=True)
    gradient = (
        lax.dot_general(
            own_columns,
            lax.all_gather(upstream, "fsdp", axis=0, tiled=True),
            (((0,), (0,)), ((), ())),
            preferred_element_type=jnp.float32,
        )
        * scaling
    )
    moment = MOMENTUM_DECAY * momentum[0] + gradient.reshape(-1, group_len)
    dct_basis = dct_rows(band_index, group_len)
    coeffs = jnp.dot(moment, dct_basis.T, precision=highest)
    leftover = (moment - jnp.dot(coeffs, dct_basis, precision=highest))[None]
    shared = lax.psum(coeffs, "rep") / lax.axis_size("rep")
    own_update = jnp.dot(shared, dct_basis, precision=highest).reshape(own_rows, width_out)
    new_weight = rebuild_rows(weight, own_update)
    running = jnp.dot(
        tok_inputs,
        lax.all_gather(new_weight, "fsdp", axis=0, tiled=True),
        preferred_element_type=jnp.float32,
    )
    values = (running * scaling).astype(jnp.bfloat16)[None]
    return (leftover, new_weight, values)


LANES = 128
F32, BF16 = jnp.float32, jnp.bfloat16


def split_hi_lo(x):
    hi = x.astype(BF16)
    return hi, (x - hi.astype(F32)).astype(BF16)


def dot(a, b, dims=((1,), (0,))):
    return lax.dot_general(a, b, (dims, ((), ())), preferred_element_type=F32)


def dot3(a_hi, a_lo, b_hi, b_lo, dims=((1,), (0,))):
    return dot(a_hi, b_hi, dims) + dot(a_hi, b_lo, dims) + dot(a_lo, b_hi, dims)


def fill_basis(band_ref, bh, bl, bt, between):
    slabs, bands, width = bh.shape
    length = slabs * width
    period = 4 * length
    freq = jnp.broadcast_to(band_ref[...].astype(F32), (LANES, bands)).T.astype(jnp.int32)
    lane = lax.broadcasted_iota(jnp.int32, (bands, LANES), 1)
    row_scale = jnp.where(freq == 0, math.sqrt(1.0 / length), math.sqrt(2.0 / length)).astype(F32)

    def angle(steps):
        centred = ((steps * freq + period // 2) & (period - 1)) - period // 2
        return centred.astype(F32) * (math.pi / (2 * length))

    fine, coarse = angle(2 * lane + 1), angle(2 * LANES * lane)
    cos_fine, sin_fine = row_scale * jnp.cos(fine), row_scale * jnp.sin(fine)
    cos_coarse, sin_coarse = jnp.cos(coarse), jnp.sin(coarse)
    between()
    for at in range(length // LANES):
        tile = cos_coarse[:, at : at + 1] * cos_fine - sin_coarse[:, at : at + 1] * sin_fine
        hi, lo = split_hi_lo(tile)
        a, col = divmod(at * LANES, width)
        bh[a, :, col : col + LANES] = hi
        bl[a, :, col : col + LANES] = lo
        hi, lo = split_hi_lo(tile.T)
        bt[at * LANES : (at + 1) * LANES, :bands] = hi
        bt[at * LANES : (at + 1) * LANES, bands:] = lo


CORE, SIDES, DIAGONAL = 1, (2, 4), 6


def kernel(
    n, reps, band_hbm, x_hbm, og_hbm, w_hbm, mom_hbm, left, nw, val,
    band, x, oc, og, w, mom, bh, bl, bt, perm, xa, zc, grad, upd, even, odd, pin, vout, vin, hout, hin,
    cl, cpo, cpi, cro, cri, cz, sg,
    load_sem, x_send, x_recv, og_send, og_recv, p_send, p_recv, v_send, h_recv, v_recv, c_send, c_recv,
    far_fsdp, far_rep,
):
    me, rep = lax.axis_index("fsdp"), lax.axis_index("rep")
    tokens, depth = x.shape
    own_rows, width = w.shape
    slabs, bands, _ = bh.shape
    groups = mom.shape[0]
    half_tokens = tokens // 2
    scaling = 1.0 / math.sqrt(depth)
    bits = n.bit_length() - 1

    def peer(k):
        return sum((((me // 2**b) % 2 + (k >> b) % 2) % 2) * 2**b for b in range(bits))

    def columns(which):
        return pl.ds(pl.multiple_of(which * own_rows, LANES), own_rows)

    def to_peer(k, src, dst, send, recv):
        return pltpu.make_async_remote_copy(
            src_ref=src, dst_ref=dst, send_sem=send, recv_sem=recv,
            device_id={"fsdp": peer(k)}, device_id_type=pl.DeviceIdType.MESH,
        )

    def to_rep(d, src, dst, send, recv):
        return pltpu.make_async_remote_copy(
            src_ref=src, dst_ref=dst, send_sem=send, recv_sem=recv,
            device_id={"rep": lax.rem(rep + d, reps)}, device_id_type=pl.DeviceIdType.MESH,
        )

    def wait_bytes(like, sem):
        pltpu.make_async_copy(like, like, sem).wait()

    def signal_peer(sem, k):
        pl.semaphore_signal(sem, inc=1, device_id={"fsdp": peer(k)}, device_id_type=pl.DeviceIdType.MESH)

    def signal_next_reps(sem):
        for there, step in ((rep > 0, -1), (rep < reps - 1, 1)):

            @pl.when(there)
            def _():
                pl.semaphore_signal(
                    sem, inc=1, device_id={"rep": rep + step}, device_id_type=pl.DeviceIdType.MESH
                )

    next_reps = (rep > 0).astype(jnp.int32) + (rep < reps - 1).astype(jnp.int32)
    barrier = pltpu.get_barrier_semaphore()
    near = [CORE] + [k + c for k in SIDES for c in (0, CORE)]
    signal_next_reps(barrier)
    for k in near:
        signal_peer(barrier, k)
    loads = [
        pltpu.make_async_copy(src, dst, load_sem.at[i])
        for i, (src, dst) in enumerate(
            (
                (band_hbm, band),
                (x_hbm.at[0], x),
                (og_hbm.at[0], og.at[0]),
                (w_hbm, w),
                (mom_hbm.at[0], mom),
                (x_hbm.at[0, :, columns(me)], oc.at[0]),
            )
        )
    ]
    for load in loads:
        load.start()
    pl.semaphore_wait(barrier, len(near) + next_reps)

    signal_peer(far_fsdp, SIDES[0])
    if reps > 2:
        signal_next_reps(far_rep.at[0])
    og_copies = {k: to_peer(k, og_hbm.at[0], og.at[k], og_send, og_recv.at[k]) for k in (*SIDES, CORE)}
    x_copies = {
        k: to_peer(k, x_hbm.at[0, :, columns(peer(k))], oc.at[k], x_send, x_recv.at[k]) for k in range(1, n)
    }
    forward = {
        k: to_peer(CORE, og.at[k], og.at[k + CORE], og_send, og_recv.at[k + CORE])
        for k in (*SIDES, DIAGONAL)
    }
    parts = [pl.ds(side * half_tokens, half_tokens) for side in range(2)]
    relays = [
        to_peer(
            SIDES[side], og.at[SIDES[1 - side], parts[side]], og.at[DIAGONAL, parts[side]],
            og_send, og_recv.at[DIAGONAL],
        )
        for side in range(2)
    ]
    for copy in og_copies.values():
        copy.start()
    x_copies[CORE].start()

    def reach_diagonal():
        pl.semaphore_wait(far_fsdp, 1)
        x_copies[DIAGONAL].start()

    loads[0].wait()
    fill_basis(band, bh, bl, bt, reach_diagonal)

    for k in SIDES:
        og_copies[k].wait_recv()
    for copy in relays:
        copy.start()
    x_copies[DIAGONAL + CORE].start()
    for k in SIDES:
        forward[k].start()

    loads[1].wait()
    span = slabs * LANES
    row = lax.broadcasted_iota(jnp.int32, (span, LANES), 0)
    lane = lax.broadcasted_iota(jnp.int32, (span, LANES), 1)
    for a in range(slabs):
        perm[:, a * LANES : (a + 1) * LANES] = (row == slabs * lane + a).astype(F32).astype(BF16)
    for piece in range(depth // span):
        sorted_piece = dot(x[:, piece * span : (piece + 1) * span], perm[...]).astype(BF16)
        for a in range(slabs):
            xa[a * tokens : (a + 1) * tokens, piece * LANES : (piece + 1) * LANES] = sorted_piece[
                :, a * LANES : (a + 1) * LANES
            ]

    loads[2].wait()
    for a in range(slabs):
        both = dot(og[0], bt[a * width : (a + 1) * width, :])
        hi, lo = split_hi_lo(both[:, :bands] + both[:, bands:])
        zc[a * tokens : (a + 1) * tokens, :bands] = hi
        zc[a * tokens : (a + 1) * tokens, bands:] = lo
    both = dot(xa[...], zc[...], ((0,), (0,)))
    cl[...] = (scaling * (both[:, :bands] + both[:, bands:])).reshape(n, groups, bands)
    for h in range(n // 2):
        cpo[h] = cl[peer(2 * h + CORE)].astype(BF16)
    pair_copy = to_peer(CORE, cpo, cpi, c_send.at[0], c_recv.at[0])
    pair_copy.start()

    def coefficients(slab_of):
        wide, narrow = None, None
        for a in range(slabs):
            hi, lo = split_hi_lo(slab_of(a))
            both = dot(hi, bt[a * width : (a + 1) * width, :])
            rest = dot(lo, bt[a * width : (a + 1) * width, :bands])
            wide = both if wide is None else wide + both
            narrow = rest if narrow is None else narrow + rest
        return wide[:, :bands] + (wide[:, bands:] + narrow)

    for load in loads[3:]:
        load.wait()
    from_momentum = coefficients(lambda a: MOMENTUM_DECAY * mom[:, a * width : (a + 1) * width])
    pair_copy.wait_recv()
    chip_copies = []
    for h in range(1, n // 2):
        cro[h] = (cl[peer(2 * h)] + cpi[h].astype(F32)).astype(BF16)
        chip_copies.append(to_peer(2 * h, cro.at[h], cri.at[h], c_send.at[1], c_recv.at[1]))
        chip_copies[-1].start()
    for k in (*SIDES, *(k + CORE for k in SIDES)):
        x_copies[k].start()
    own_sum = from_momentum + (cl[me] + cpi[0].astype(F32))
    if reps > 2:
        for at in range(reps - 3):
            pl.semaphore_wait(far_rep.at[at], next_reps)
            signal_next_reps(far_rep.at[at + 1])

    tiles = range(width // LANES)
    first = dot(oc[0], og[0], ((0,), (0,)))
    for t in tiles:
        grad[t] = first[:, t * LANES : (t + 1) * LANES]
    even[0] = dot(oc[0], w[...])
    to_partner = {}

    def take(k):
        x_copies[k].wait_recv()
        partial = dot(oc[k], w[...])
        if k % 2:
            odd[k // 2] = partial.astype(BF16)
            to_partner[k] = to_peer(CORE, odd.at[k // 2], pin.at[k // 2], p_send, p_recv.at[k // 2])
            to_partner[k].start()
        else:
            even[k // 2] = partial
        if k == CORE:
            og_copies[CORE].wait_recv()
        elif k % 2:
            forward[k - CORE].wait_recv()
        product = dot(oc[k], og[k], ((0,), (0,)))
        for t in tiles:
            grad[t] += product[:, t * LANES : (t + 1) * LANES]

    take(CORE)
    wait_bytes(og.at[DIAGONAL], og_recv.at[DIAGONAL])
    forward[DIAGONAL].start()
    take(DIAGONAL)
    take(DIAGONAL + CORE)

    wait_bytes(cri.at[1 : n // 2], c_recv.at[1])
    for h in range(1, n // 2):
        own_sum = own_sum + cri[h].astype(F32)
    cz[rep] = own_sum.astype(BF16)
    if reps > 2:
        pl.semaphore_wait(far_rep.at[reps - 3], next_reps)
    for d in range(1, reps):
        to_rep(d, cz.at[rep], cz.at[rep], c_send.at[2], c_recv.at[2]).start()

    to_partner[DIAGONAL + CORE].wait_recv()
    across = even[DIAGONAL // 2] + pin[DIAGONAL // 2].astype(F32)
    halves = []
    for side, k in enumerate(SIDES):
        hout[side] = across[side * half_tokens : (side + 1) * half_tokens].astype(BF16)
        halves.append(to_peer(k, hout.at[side], hin.at[side], v_send, h_recv.at[side]))
        halves[-1].start()
    take(SIDES[0])
    take(SIDES[1])

    wait_bytes(cz.at[: reps - 1], c_recv.at[2])
    shared = cz[0].astype(F32)
    for d in range(1, reps):
        shared = shared + cz[d].astype(F32)
    shared = shared / reps
    sg[me] = shared.astype(BF16)
    for k in (*SIDES, DIAGONAL):
        to_peer(k, sg.at[me], sg.at[me], c_send.at[3], c_recv.at[3]).start()
    to_peer(CORE, sg.at[me], sg.at[me], c_send.at[3], c_recv.at[4]).start()
    take(SIDES[0] + CORE)
    take(SIDES[1] + CORE)

    v_copies = []
    for side, k in enumerate(SIDES):
        to_partner[k + CORE].wait_recv()
        halves[1 - side].wait_recv()
        both = even[k // 2] + pin[k // 2].astype(F32)
        cut = slice((1 - side) * half_tokens, (2 - side) * half_tokens)
        same = slice(side * half_tokens, (side + 1) * half_tokens)
        vout[side, same] = both[same].astype(BF16)
        vout[side, cut] = (both[cut] + hin[1 - side].astype(F32)).astype(BF16)
        v_copies.append(to_peer(k, vout.at[side], vin.at[side], v_send, v_recv.at[side]))
        v_copies[-1].start()

    wait_bytes(sg.at[:3], c_recv.at[3])
    for k in (*SIDES, DIAGONAL):
        to_peer(CORE, sg.at[peer(k)], sg.at[peer(k)], c_send.at[3], c_recv.at[4]).start()

    def gradient_slab(a):
        rows = [grad[t, pl.ds(a, groups, stride=slabs), :] for t in tiles]
        return scaling * jnp.concatenate(rows, 1)

    def keep_moment(a):
        part = gradient_slab(a)
        cut = slice(a * width, (a + 1) * width)
        mom[:, cut] = MOMENTUM_DECAY * mom[:, cut] + part
        return part

    c_hi, c_lo = split_hi_lo(from_momentum + coefficients(keep_moment))
    for a in range(slabs):
        cut = slice(a * width, (a + 1) * width)
        left[0, :, cut] = mom[:, cut] - dot3(c_hi, c_lo, bh[a], bl[a])

    s_hi, s_lo = split_hi_lo(shared)
    for a in range(slabs):
        product = dot3(s_hi, s_lo, bh[a], bl[a])
        for t in tiles:
            upd[t, pl.ds(a, groups, stride=slabs), :] = product[:, t * LANES : (t + 1) * LANES]
    for t in tiles:
        cut = slice(t * LANES, (t + 1) * LANES)
        nw[:, cut] = rebuild_rows(w[:, cut], upd[t])

    wait_bytes(sg.at[:4], c_recv.at[4])
    mixed = dot(xa[...], sg[...].reshape(n * groups, bands))
    mixed = jnp.concatenate([mixed[a * tokens : (a + 1) * tokens] for a in range(slabs)], 1)
    hi, lo = split_hi_lo(mixed)
    change = dot3(hi, lo, bh[...].reshape(slabs * bands, width), bl[...].reshape(slabs * bands, width))
    to_partner[CORE].wait_recv()
    base = even[0] + pin[0].astype(F32) - LEARNING_RATE * change
    for copy in v_copies:
        copy.wait_recv()
    for side in range(2):
        base = base + vin[side].astype(F32)
    val[0] = (base * scaling).astype(BF16)

    wait_bytes(oc.at[1:], x_send)
    wait_bytes(og.at[1:], og_send)
    wait_bytes(odd, p_send)
    wait_bytes(odd.at[:3], v_send)
    wait_bytes(cpo, c_send.at[0])
    wait_bytes(cri.at[1:], c_send.at[1])
    wait_bytes(cz.at[: reps - 1], c_send.at[2])
    wait_bytes(sg.at[:7], c_send.at[3])


def store_kernel(left, nw, val, left_hbm, nw_hbm, val_hbm, sems):
    copies = [
        pltpu.make_async_copy(src, dst, sems.at[i])
        for i, (src, dst) in enumerate(((left, left_hbm), (nw, nw_hbm), (val, val_hbm)))
    ]
    for copy in copies:
        copy.start()
    for copy in copies:
        copy.wait()


def fused_shards(n, reps, inputs, out_grad, weight, momentum, band_index):
    tokens, depth = inputs.shape[1:]
    own_rows, width = weight.shape
    groups, group_len = momentum.shape[1:]
    slabs, bands = group_len // width, band_index.shape[0]
    half = n // 2
    dma, regular = pltpu.SemaphoreType.DMA, pltpu.SemaphoreType.REGULAR
    span = slabs * LANES
    anywhere = pl.BlockSpec(memory_space=pl.ANY)
    held = pl.pallas_call(
        functools.partial(kernel, n, reps),
        out_shape=(
            pltpu.VMEM(momentum.shape, F32),
            pltpu.VMEM(weight.shape, BF16),
            pltpu.VMEM(out_grad.shape, BF16),
        ),
        in_specs=[anywhere] * 5,
        out_specs=(pl.BlockSpec(memory_space=pltpu.VMEM),) * 3,
        scratch_shapes=[
            pltpu.VMEM((1, bands), jnp.int32),
            pltpu.VMEM((tokens, depth), BF16),
            pltpu.VMEM((n, tokens, own_rows), BF16),
            pltpu.VMEM((n, tokens, width), BF16),
            pltpu.VMEM((own_rows, width), BF16),
            pltpu.VMEM((groups, group_len), F32),
            pltpu.VMEM((slabs, bands, width), BF16),
            pltpu.VMEM((slabs, bands, width), BF16),
            pltpu.VMEM((group_len, 2 * bands), BF16),
            pltpu.VMEM((span, span), BF16),
            pltpu.VMEM((slabs * tokens, depth // slabs), BF16),
            pltpu.VMEM((slabs * tokens, 2 * bands), BF16),
            pltpu.VMEM((width // LANES, own_rows, LANES), F32),
            pltpu.VMEM((width // LANES, own_rows, LANES), F32),
            pltpu.VMEM((half, tokens, width), F32),
            pltpu.VMEM((half, tokens, width), BF16),
            pltpu.VMEM((half, tokens, width), BF16),
            pltpu.VMEM((2, tokens, width), BF16),
            pltpu.VMEM((2, tokens, width), BF16),
            pltpu.VMEM((2, tokens // 2, width), BF16),
            pltpu.VMEM((2, tokens // 2, width), BF16),
            pltpu.VMEM((n, groups, bands), F32),
            pltpu.VMEM((half, groups, bands), BF16),
            pltpu.VMEM((half, groups, bands), BF16),
            pltpu.VMEM((half, groups, bands), BF16),
            pltpu.VMEM((half, groups, bands), BF16),
            pltpu.VMEM((reps, groups, bands), BF16),
            pltpu.VMEM((n, groups, bands), BF16),
            dma((6,)),
            dma, dma((n,)), dma, dma((n,)), dma, dma((half,)), dma, dma((2,)), dma((2,)),
            dma((4,)), dma((5,)),
            regular, regular((max(reps - 2, 1),)),
        ],
        compiler_params=pltpu.CompilerParams(collective_id=0, has_side_effects=True),
    )(band_index.reshape(1, -1), inputs, out_grad, weight, momentum)
    return pl.pallas_call(
        store_kernel,
        out_shape=tuple(jax.ShapeDtypeStruct(a.shape, a.dtype) for a in held),
        in_specs=[anywhere] * 3,
        out_specs=(anywhere,) * 3,
        scratch_shapes=[dma((3,))],
        compiler_params=pltpu.CompilerParams(vmem_limit_bytes=1 << 20),
    )(*held)


def fits_kernel(n, reps, inputs, weight, momentum, band_index):
    tokens, depth = inputs.shape[1:]
    own_rows, width = weight.shape
    groups, group_len = momentum.shape[1:]
    return (
        n == CORE + DIAGONAL + 1
        and reps > 1
        and group_len & (group_len - 1) == 0
        and tokens % 32 == 0
        and own_rows % LANES == 0
        and width % LANES == 0
        and groups % 16 == 0
        and group_len % width == 0
        and group_len // LANES <= LANES
        and depth % (group_len // width * LANES) == 0
        and n * groups * (group_len // width) == depth
        and band_index.shape[0] % LANES == 0
    )


def program(n, reps, inputs, out_grad, weight, momentum, band_index):
    if fits_kernel(n, reps, inputs, weight, momentum, band_index):
        return fused_shards(n, reps, inputs, out_grad, weight, momentum, band_index)
    return shards(inputs, out_grad, weight, momentum, band_index)


def solution(mesh):
    placed = (
        P("rep", "fsdp", None),
        P("rep", "fsdp", None),
        P("fsdp", None),
        P("rep", "fsdp", None),
        P(),
    )
    return jax.shard_map(
        functools.partial(program, mesh.shape["fsdp"], mesh.shape["rep"]),
        mesh=mesh,
        in_specs=placed,
        out_specs=(P("rep", "fsdp", None), P("fsdp", None), P("rep", "fsdp", None)),
        check_vma=False,
    )
```

```python
import functools
import math

import jax
import jax.numpy as jnp
from jax import lax
from jax.experimental import pallas as pl
from jax.experimental.pallas import tpu as pltpu
from jax.sharding import PartitionSpec as P

MOMENTUM_DECAY = 0.9
LEARNING_RATE = 4.0


def dct_rows(band_index, length):
    positions = lax.iota(jnp.int32, length)
    phase_int = (2 * positions[None, :] + 1) * band_index[:, None] % (4 * length)
    angles = phase_int.astype(jnp.float32) * (math.pi / (2 * length))
    row_scale = jnp.where(band_index == 0, math.sqrt(1.0 / length), math.sqrt(2.0 / length)).astype(
        jnp.float32
    )
    return row_scale[:, None] * jnp.cos(angles)


def rebuild_rows(old_rows, update_rows):
    return (old_rows.astype(jnp.float32) - LEARNING_RATE * update_rows).astype(jnp.bfloat16)


def shards(inputs, out_grad, weight, momentum, band_index):
    tok_inputs = inputs[0]
    upstream = out_grad[0]
    own_rows = weight.shape[0]
    width_out = weight.shape[1]
    group_len = momentum.shape[2]
    scaling = 1.0 / math.sqrt(tok_inputs.shape[1])
    highest = lax.Precision.HIGHEST
    own_columns = lax.all_to_all(tok_inputs, "fsdp", split_axis=1, concat_axis=0, tiled=True)
    gradient = (
        lax.dot_general(
            own_columns,
            lax.all_gather(upstream, "fsdp", axis=0, tiled=True),
            (((0,), (0,)), ((), ())),
            preferred_element_type=jnp.float32,
        )
        * scaling
    )
    moment = MOMENTUM_DECAY * momentum[0] + gradient.reshape(-1, group_len)
    dct_basis = dct_rows(band_index, group_len)
    coeffs = jnp.dot(moment, dct_basis.T, precision=highest)
    leftover = (moment - jnp.dot(coeffs, dct_basis, precision=highest))[None]
    shared = lax.psum(coeffs, "rep") / lax.axis_size("rep")
    own_update = jnp.dot(shared, dct_basis, precision=highest).reshape(own_rows, width_out)
    new_weight = rebuild_rows(weight, own_update)
    running = jnp.dot(
        tok_inputs,
        lax.all_gather(new_weight, "fsdp", axis=0, tiled=True),
        preferred_element_type=jnp.float32,
    )
    values = (running * scaling).astype(jnp.bfloat16)[None]
    return (leftover, new_weight, values)


LANES = 128
F32, BF16 = jnp.float32, jnp.bfloat16


def split_hi_lo(x):
    hi = x.astype(BF16)
    return hi, (x - hi.astype(F32)).astype(BF16)


def dot(a, b, dims=((1,), (0,))):
    return lax.dot_general(a, b, (dims, ((), ())), preferred_element_type=F32)


def doubled(x):
    hi, lo = split_hi_lo(x)
    return jnp.concatenate([jnp.concatenate([part, part], 1) for part in (hi, lo)], 0)


def fill_basis(band_ref, bw, bt, between):
    slabs, bands, width = bw.shape
    bands //= 2
    length = slabs * width
    period = 4 * length
    freq = jnp.broadcast_to(band_ref[...].astype(F32), (LANES, bands)).T.astype(jnp.int32)
    lane = lax.broadcasted_iota(jnp.int32, (bands, LANES), 1)
    row_scale = jnp.where(freq == 0, math.sqrt(1.0 / length), math.sqrt(2.0 / length)).astype(F32)

    def angle(steps):
        centred = ((steps * freq + period // 2) & (period - 1)) - period // 2
        return centred.astype(F32) * (math.pi / (2 * length))

    fine, coarse = angle(2 * lane + 1), angle(2 * LANES * lane)
    cos_fine, sin_fine = row_scale * jnp.cos(fine), row_scale * jnp.sin(fine)
    cos_coarse, sin_coarse = jnp.cos(coarse), jnp.sin(coarse)
    between()
    for at in range(length // LANES):
        tile = cos_coarse[:, at : at + 1] * cos_fine - sin_coarse[:, at : at + 1] * sin_fine
        hi, lo = split_hi_lo(tile)
        a, col = divmod(at * LANES, width)
        bw[a, :bands, col : col + LANES] = hi
        bw[a, bands:, col : col + LANES] = lo
        hi, lo = split_hi_lo(tile.T)
        bt[at * LANES : (at + 1) * LANES, :bands] = hi
        bt[at * LANES : (at + 1) * LANES, bands:] = lo


CORE, SIDES, DIAGONAL = 1, (2, 4), 6


def kernel(
    n, reps, band_hbm, x_hbm, og_hbm, w_hbm, mom_hbm, left, nw, val,
    band, x, oc, og, w, mom, bw, bt, perm, xa, zc, grad, upd, even, odd, pin, vout, vin, hout, hin,
    cl, cpo, cpi, cro, cri, cz, sg,
    load_sem, x_send, x_recv, last_recv, og_send, og_recv, p_send, p_recv, v_send, h_recv, v_recv, c_send, c_recv,
    side_entered, rep_round, all_entered,
):
    me, rep = lax.axis_index("fsdp"), lax.axis_index("rep")
    tokens, depth = x.shape
    own_rows, width = w.shape
    slabs, bands = bw.shape[0], bw.shape[1] // 2
    groups = mom.shape[0]
    half_tokens = tokens // 2
    scaling = 1.0 / math.sqrt(depth)
    bits = n.bit_length() - 1

    def peer(k):
        return sum((((me // 2**b) % 2 + (k >> b) % 2) % 2) * 2**b for b in range(bits))

    def columns(which):
        return pl.ds(pl.multiple_of(which * own_rows, LANES), own_rows)

    def to_peer(k, src, dst, send, recv):
        return pltpu.make_async_remote_copy(
            src_ref=src, dst_ref=dst, send_sem=send, recv_sem=recv,
            device_id={"fsdp": peer(k)}, device_id_type=pl.DeviceIdType.MESH,
        )

    def to_rep(d, src, dst, send, recv):
        return pltpu.make_async_remote_copy(
            src_ref=src, dst_ref=dst, send_sem=send, recv_sem=recv,
            device_id={"rep": lax.rem(rep + d, reps)}, device_id_type=pl.DeviceIdType.MESH,
        )

    def wait_bytes(like, sem):
        pltpu.make_async_copy(like, like, sem).wait()

    def signal_peer(sem, k):
        pl.semaphore_signal(sem, inc=1, device_id={"fsdp": peer(k)}, device_id_type=pl.DeviceIdType.MESH)

    first = me == 0

    def signal_next_reps(sem):
        for there, step in ((rep > 0, -1), (rep < reps - 1, 1)):

            @pl.when(first & there)
            def _():
                pl.semaphore_signal(
                    sem, inc=1, device_id={"rep": rep + step}, device_id_type=pl.DeviceIdType.MESH
                )

    next_reps = (rep > 0).astype(jnp.int32) + (rep < reps - 1).astype(jnp.int32)

    def pass_on(at):
        @pl.when(first)
        def _():
            pl.semaphore_wait(rep_round.at[at], next_reps)

        if at + 1 < reps - 1:
            signal_next_reps(rep_round.at[at + 1])
            return
        for k in range(1, n):

            @pl.when(first)
            def _():
                signal_peer(all_entered, k)

    barrier = pltpu.get_barrier_semaphore()
    near = [CORE] + [k + c for k in SIDES for c in (0, CORE)]
    signal_next_reps(barrier)
    for k in near:
        signal_peer(barrier, k)
    loads = [
        pltpu.make_async_copy(src, dst, load_sem.at[i])
        for i, (src, dst) in enumerate(
            (
                (band_hbm, band),
                (x_hbm.at[0], x),
                (og_hbm.at[0], og.at[0]),
                (w_hbm, w),
                (mom_hbm.at[0], mom),
                (x_hbm.at[0, :, columns(me)], oc.at[0]),
            )
        )
    ]
    for load in loads:
        load.start()
    pl.semaphore_wait(barrier, len(near) + jnp.where(first, next_reps, 0))

    signal_peer(side_entered, SIDES[0])
    og_copies = {k: to_peer(k, og_hbm.at[0], og.at[k], og_send, og_recv.at[k]) for k in (*SIDES, CORE)}
    x_copies = {
        k: to_peer(k, x_hbm.at[0, :, columns(peer(k))], oc.at[k], x_send, x_recv.at[k])
        for k in range(1, n)
        if k not in SIDES
    }
    parts = [pl.ds(side * half_tokens, half_tokens) for side in range(2)]
    last_copies = {
        (k, part): to_peer(
            k, x_hbm.at[0, parts[part], columns(peer(k))], oc.at[k, parts[part]], x_send, last_recv.at[i, part]
        )
        for i, k in enumerate(SIDES)
        for part in range(2)
    }
    forward = {
        k: to_peer(CORE, og.at[k], og.at[k + CORE], og_send, og_recv.at[k + CORE])
        for k in (*SIDES, DIAGONAL)
    }
    relays = [
        to_peer(
            SIDES[side], og.at[SIDES[1 - side], parts[side]], og.at[DIAGONAL, parts[side]],
            og_send, og_recv.at[DIAGONAL],
        )
        for side in range(2)
    ]
    for copy in og_copies.values():
        copy.start()
    x_copies[CORE].start()

    def reach_diagonal():
        pl.semaphore_wait(side_entered, 1)
        x_copies[DIAGONAL].start()
        signal_next_reps(rep_round.at[0])

    loads[0].wait()
    fill_basis(band, bw, bt, reach_diagonal)

    pass_on(0)
    loads[1].wait()
    span = slabs * LANES
    row = lax.broadcasted_iota(jnp.int32, (span, LANES), 0)
    lane = lax.broadcasted_iota(jnp.int32, (span, LANES), 1)
    for a in range(slabs):
        perm[:, a * LANES : (a + 1) * LANES] = (row == slabs * lane + a).astype(F32).astype(BF16)
    for piece in range(depth // span):
        sorted_piece = dot(x[:, piece * span : (piece + 1) * span], perm[...]).astype(BF16)
        for a in range(slabs):
            xa[a * tokens : (a + 1) * tokens, piece * LANES : (piece + 1) * LANES] = sorted_piece[
                :, a * LANES : (a + 1) * LANES
            ]

    loads[2].wait()
    for a in range(slabs):
        both = dot(og[0], bt[a * width : (a + 1) * width, :])
        hi, lo = split_hi_lo(both[:, :bands] + both[:, bands:])
        zc[a * tokens : (a + 1) * tokens, :bands] = hi
        zc[a * tokens : (a + 1) * tokens, bands:] = lo
    both = dot(xa[...], zc[...], ((0,), (0,)))
    cl[...] = (scaling * (both[:, :bands] + both[:, bands:])).reshape(n, groups, bands)
    for h in range(n // 2):
        cpo[h] = cl[peer(2 * h + CORE)].astype(BF16)
    pair_copy = to_peer(CORE, cpo, cpi, c_send.at[0], c_recv.at[0])
    pair_copy.start()

    pass_on(1)
    for k in SIDES:
        og_copies[k].wait_recv()
    for copy in relays:
        copy.start()
    for k in SIDES:
        forward[k].start()

    def coefficients(slab_of):
        both = None
        for a in range(slabs):
            stacked = jnp.concatenate(split_hi_lo(slab_of(a)), 0)
            product = dot(stacked, bt[a * width : (a + 1) * width, :])
            both = product if both is None else both + product
        both = both[:, :bands] + both[:, bands:]
        return both[:groups] + both[groups:]

    def expand(stacked, a):
        both = dot(stacked, bw[a])
        return both[:groups] + both[groups:]

    for load in loads[3:]:
        load.wait()
    tiles = range(width // LANES)
    product = dot(oc[0], og[0], ((0,), (0,)))
    for t in tiles:
        grad[t] = product[:, t * LANES : (t + 1) * LANES]
    even[0] = dot(oc[0], w[...])
    to_partner = {}

    def take_values(k):
        x_copies[k].wait_recv()
        partial = dot(oc[k], w[...])
        if k % 2:
            odd[k // 2] = partial.astype(BF16)
            to_partner[k] = to_peer(CORE, odd.at[k // 2], pin.at[k // 2], p_send, p_recv.at[k // 2])
            to_partner[k].start()
        else:
            even[k // 2] = partial

    def take_gradient(k):
        if k == CORE:
            og_copies[CORE].wait_recv()
        elif k % 2:
            forward[k - CORE].wait_recv()
        product = dot(oc[k], og[k], ((0,), (0,)))
        for t in tiles:
            grad[t] += product[:, t * LANES : (t + 1) * LANES]

    def take(k):
        take_values(k)
        take_gradient(k)

    take(CORE)
    pair_copy.wait_recv()
    for h in range(1, n // 2):
        cro[h] = (cl[peer(2 * h)] + cpi[h].astype(F32)).astype(BF16)
        to_peer(2 * h, cro.at[h], cri.at[h], c_send.at[1], c_recv.at[1]).start()
    from_momentum = coefficients(lambda a: MOMENTUM_DECAY * mom[:, a * width : (a + 1) * width])
    own_sum = from_momentum + (cl[me] + cpi[0].astype(F32))
    for k in (DIAGONAL + CORE, *(k + CORE for k in SIDES)):
        x_copies[k].start()
    for at in range(2, reps - 1):
        pass_on(at)
    take_values(DIAGONAL)
    wait_bytes(cri.at[1 : n // 2], c_recv.at[1])
    for h in range(1, n // 2):
        own_sum = own_sum + cri[h].astype(F32)
    cz[rep] = own_sum.astype(BF16)

    @pl.when(jnp.logical_not(first))
    def _():
        pl.semaphore_wait(all_entered, 1)

    for d in range(1, reps):
        to_rep(d, cz.at[rep], cz.at[rep], c_send.at[2], c_recv.at[2]).start()

    wait_bytes(og.at[DIAGONAL], og_recv.at[DIAGONAL])
    forward[DIAGONAL].start()
    take_gradient(DIAGONAL)
    for k in SIDES:
        last_copies[k, 0].start()
    take(DIAGONAL + CORE)
    to_partner[DIAGONAL + CORE].wait_recv()
    across = even[DIAGONAL // 2] + pin[DIAGONAL // 2].astype(F32)
    halves = []
    for side, k in enumerate(SIDES):
        hout[side] = across[side * half_tokens : (side + 1) * half_tokens].astype(BF16)
        halves.append(to_peer(k, hout.at[side], hin.at[side], v_send, h_recv.at[side]))
        halves[-1].start()
    for k in SIDES:
        last_copies[k, 1].start()
    take(SIDES[0] + CORE)
    take(SIDES[1] + CORE)

    wait_bytes(cz.at[: reps - 1], c_recv.at[2])
    shared = cz[0].astype(F32)
    for d in range(1, reps):
        shared = shared + cz[d].astype(F32)
    shared = shared / reps
    sg[me] = shared.astype(BF16)
    for k in (*SIDES, DIAGONAL):
        to_peer(k, sg.at[me], sg.at[me], c_send.at[3], c_recv.at[3]).start()
    to_peer(CORE, sg.at[me], sg.at[me], c_send.at[3], c_recv.at[4]).start()
    agreed = doubled(shared)
    for a in range(slabs):
        product = expand(agreed, a)
        for t in tiles:
            upd[t, pl.ds(a, groups, stride=slabs), :] = product[:, t * LANES : (t + 1) * LANES]
    for t in tiles:
        cut = slice(t * LANES, (t + 1) * LANES)
        nw[:, cut] = rebuild_rows(w[:, cut], upd[t])

    v_copies = []
    for part in range(2):
        cut = slice(part * half_tokens, (part + 1) * half_tokens)
        for side, k in enumerate(SIDES):
            last_copies[k, part].wait_recv()
            ours = dot(oc[k, cut], w[...])
            if part == 0:
                to_partner[k + CORE].wait_recv()
            ours = ours + pin[k // 2, cut].astype(F32)
            if part != side:
                halves[part].wait_recv()
                ours = ours + hin[part].astype(F32)
            vout[side, cut] = ours.astype(BF16)
            v_copies.append(
                to_peer(k, vout.at[side, parts[part]], vin.at[side, parts[part]], v_send, v_recv.at[side, part])
            )
            v_copies[-1].start()
    wait_bytes(sg.at[:3], c_recv.at[3])
    for k in (*SIDES, DIAGONAL):
        to_peer(CORE, sg.at[peer(k)], sg.at[peer(k)], c_send.at[3], c_recv.at[4]).start()
    for k in SIDES:
        take_gradient(k)

    def gradient_slab(a):
        rows = [grad[t, pl.ds(a, groups, stride=slabs), :] for t in tiles]
        return scaling * jnp.concatenate(rows, 1)

    def keep_moment(a):
        part = gradient_slab(a)
        cut = slice(a * width, (a + 1) * width)
        mom[:, cut] = MOMENTUM_DECAY * mom[:, cut] + part
        return part

    kept = doubled(from_momentum + coefficients(keep_moment))
    for a in range(slabs):
        cut = slice(a * width, (a + 1) * width)
        left[0, :, cut] = mom[:, cut] - expand(kept, a)

    wait_bytes(sg.at[:4], c_recv.at[4])
    mixed = dot(xa[...], sg[...].reshape(n * groups, bands))
    mixed = jnp.concatenate([doubled(mixed[a * tokens : (a + 1) * tokens]) for a in range(slabs)], 1)
    change = dot(mixed, bw[...].reshape(2 * slabs * bands, width))
    change = change[:tokens] + change[tokens:]
    to_partner[CORE].wait_recv()
    base = even[0] + pin[0].astype(F32) - LEARNING_RATE * change
    for copy in v_copies:
        copy.wait_recv()
    for side in range(2):
        base = base + vin[side].astype(F32)
    val[0] = (base * scaling).astype(BF16)

    wait_bytes(oc.at[1:], x_send)
    wait_bytes(og.at[1:], og_send)
    wait_bytes(odd, p_send)
    wait_bytes(odd.at[:3], v_send)
    wait_bytes(cpo, c_send.at[0])
    wait_bytes(cri.at[1:], c_send.at[1])
    wait_bytes(cz.at[: reps - 1], c_send.at[2])
    wait_bytes(sg.at[:7], c_send.at[3])


def store_kernel(left, nw, val, left_hbm, nw_hbm, val_hbm, sems):
    copies = [
        pltpu.make_async_copy(src, dst, sems.at[i])
        for i, (src, dst) in enumerate(((left, left_hbm), (nw, nw_hbm), (val, val_hbm)))
    ]
    for copy in copies:
        copy.start()
    for copy in copies:
        copy.wait()


def fused_shards(n, reps, inputs, out_grad, weight, momentum, band_index):
    tokens, depth = inputs.shape[1:]
    own_rows, width = weight.shape
    groups, group_len = momentum.shape[1:]
    slabs, bands = group_len // width, band_index.shape[0]
    half = n // 2
    dma, regular = pltpu.SemaphoreType.DMA, pltpu.SemaphoreType.REGULAR
    span = slabs * LANES
    anywhere = pl.BlockSpec(memory_space=pl.ANY)
    held = pl.pallas_call(
        functools.partial(kernel, n, reps),
        out_shape=(
            pltpu.VMEM(momentum.shape, F32),
            pltpu.VMEM(weight.shape, BF16),
            pltpu.VMEM(out_grad.shape, BF16),
        ),
        in_specs=[anywhere] * 5,
        out_specs=(pl.BlockSpec(memory_space=pltpu.VMEM),) * 3,
        scratch_shapes=[
            pltpu.VMEM((1, bands), jnp.int32),
            pltpu.VMEM((tokens, depth), BF16),
            pltpu.VMEM((n, tokens, own_rows), BF16),
            pltpu.VMEM((n, tokens, width), BF16),
            pltpu.VMEM((own_rows, width), BF16),
            pltpu.VMEM((groups, group_len), F32),
            pltpu.VMEM((slabs, 2 * bands, width), BF16),
            pltpu.VMEM((group_len, 2 * bands), BF16),
            pltpu.VMEM((span, span), BF16),
            pltpu.VMEM((slabs * tokens, depth // slabs), BF16),
            pltpu.VMEM((slabs * tokens, 2 * bands), BF16),
            pltpu.VMEM((width // LANES, own_rows, LANES), F32),
            pltpu.VMEM((width // LANES, own_rows, LANES), F32),
            pltpu.VMEM((half, tokens, width), F32),
            pltpu.VMEM((half, tokens, width), BF16),
            pltpu.VMEM((half, tokens, width), BF16),
            pltpu.VMEM((2, tokens, width), BF16),
            pltpu.VMEM((2, tokens, width), BF16),
            pltpu.VMEM((2, tokens // 2, width), BF16),
            pltpu.VMEM((2, tokens // 2, width), BF16),
            pltpu.VMEM((n, groups, bands), F32),
            pltpu.VMEM((half, groups, bands), BF16),
            pltpu.VMEM((half, groups, bands), BF16),
            pltpu.VMEM((half, groups, bands), BF16),
            pltpu.VMEM((half, groups, bands), BF16),
            pltpu.VMEM((reps, groups, bands), BF16),
            pltpu.VMEM((n, groups, bands), BF16),
            dma((6,)),
            dma, dma((n,)), dma((2, 2)), dma, dma((n,)), dma, dma((half,)), dma, dma((2,)), dma((2, 2)),
            dma((4,)), dma((5,)),
            regular, regular((reps - 1,)), regular,
        ],
        compiler_params=pltpu.CompilerParams(collective_id=0, has_side_effects=True),
    )(band_index.reshape(1, -1), inputs, out_grad, weight, momentum)
    return pl.pallas_call(
        store_kernel,
        out_shape=tuple(jax.ShapeDtypeStruct(a.shape, a.dtype) for a in held),
        in_specs=[anywhere] * 3,
        out_specs=(anywhere,) * 3,
        scratch_shapes=[dma((3,))],
        compiler_params=pltpu.CompilerParams(vmem_limit_bytes=1 << 20),
    )(*held)


def fits_kernel(n, reps, inputs, weight, momentum, band_index):
    tokens, depth = inputs.shape[1:]
    own_rows, width = weight.shape
    groups, group_len = momentum.shape[1:]
    return (
        n == CORE + DIAGONAL + 1
        and reps > 1
        and group_len & (group_len - 1) == 0
        and tokens % 32 == 0
        and own_rows % LANES == 0
        and width % LANES == 0
        and groups % 16 == 0
        and group_len % width == 0
        and group_len // LANES <= LANES
        and depth % (group_len // width * LANES) == 0
        and n * groups * (group_len // width) == depth
        and band_index.shape[0] % LANES == 0
    )


def program(n, reps, inputs, out_grad, weight, momentum, band_index):
    if fits_kernel(n, reps, inputs, weight, momentum, band_index):
        return fused_shards(n, reps, inputs, out_grad, weight, momentum, band_index)
    return shards(inputs, out_grad, weight, momentum, band_index)


def solution(mesh):
    placed = (
        P("rep", "fsdp", None),
        P("rep", "fsdp", None),
        P("fsdp", None),
        P("rep", "fsdp", None),
        P(),
    )
    return jax.shard_map(
        functools.partial(program, mesh.shape["fsdp"], mesh.shape["rep"]),
        mesh=mesh,
        in_specs=placed,
        out_specs=(P("rep", "fsdp", None), P("fsdp", None), P("rep", "fsdp", None)),
        check_vma=False,
    )
```

```python
import functools
import math

import jax
import jax.numpy as jnp
from jax import lax
from jax.experimental import pallas as pl
from jax.experimental.pallas import tpu as pltpu
from jax.sharding import PartitionSpec as P

MOMENTUM_DECAY = 0.9
LEARNING_RATE = 4.0


def dct_rows(band_index, length):
    positions = lax.iota(jnp.int32, length)
    phase_int = (2 * positions[None, :] + 1) * band_index[:, None] % (4 * length)
    angles = phase_int.astype(jnp.float32) * (math.pi / (2 * length))
    row_scale = jnp.where(band_index == 0, math.sqrt(1.0 / length), math.sqrt(2.0 / length)).astype(
        jnp.float32
    )
    return row_scale[:, None] * jnp.cos(angles)


def rebuild_rows(old_rows, update_rows):
    return (old_rows.astype(jnp.float32) - LEARNING_RATE * update_rows).astype(jnp.bfloat16)


def shards(inputs, out_grad, weight, momentum, band_index):
    tok_inputs = inputs[0]
    upstream = out_grad[0]
    own_rows = weight.shape[0]
    width_out = weight.shape[1]
    group_len = momentum.shape[2]
    scaling = 1.0 / math.sqrt(tok_inputs.shape[1])
    highest = lax.Precision.HIGHEST
    own_columns = lax.all_to_all(tok_inputs, "fsdp", split_axis=1, concat_axis=0, tiled=True)
    gradient = (
        lax.dot_general(
            own_columns,
            lax.all_gather(upstream, "fsdp", axis=0, tiled=True),
            (((0,), (0,)), ((), ())),
            preferred_element_type=jnp.float32,
        )
        * scaling
    )
    moment = MOMENTUM_DECAY * momentum[0] + gradient.reshape(-1, group_len)
    dct_basis = dct_rows(band_index, group_len)
    coeffs = jnp.dot(moment, dct_basis.T, precision=highest)
    leftover = (moment - jnp.dot(coeffs, dct_basis, precision=highest))[None]
    shared = lax.psum(coeffs, "rep") / lax.axis_size("rep")
    own_update = jnp.dot(shared, dct_basis, precision=highest).reshape(own_rows, width_out)
    new_weight = rebuild_rows(weight, own_update)
    running = jnp.dot(
        tok_inputs,
        lax.all_gather(new_weight, "fsdp", axis=0, tiled=True),
        preferred_element_type=jnp.float32,
    )
    values = (running * scaling).astype(jnp.bfloat16)[None]
    return (leftover, new_weight, values)


LANES = 128
F32, BF16 = jnp.float32, jnp.bfloat16


def split_hi_lo(x):
    hi = x.astype(BF16)
    return hi, (x - hi.astype(F32)).astype(BF16)


def dot(a, b, dims=((1,), (0,))):
    return lax.dot_general(a, b, (dims, ((), ())), preferred_element_type=F32)


def doubled(x):
    hi, lo = split_hi_lo(x)
    return jnp.concatenate([jnp.concatenate([part, part], 1) for part in (hi, lo)], 0)


def fill_basis(band_ref, bw, bt, before, beside):
    slabs, bands, width = bw.shape
    bands //= 2
    length = slabs * width
    period = 4 * length
    freq = jnp.broadcast_to(band_ref[...].astype(F32), (LANES, bands)).T.astype(jnp.int32)
    lane = lax.broadcasted_iota(jnp.int32, (bands, LANES), 1)
    row_scale = jnp.where(freq == 0, math.sqrt(1.0 / length), math.sqrt(2.0 / length)).astype(F32)

    def angle(steps):
        centred = ((steps * freq + period // 2) & (period - 1)) - period // 2
        return centred.astype(F32) * (math.pi / (2 * length))

    fine, coarse = angle(2 * lane + 1), angle(2 * LANES * lane)
    cos_fine, sin_fine = row_scale * jnp.cos(fine), row_scale * jnp.sin(fine)
    cos_coarse, sin_coarse = jnp.cos(coarse), jnp.sin(coarse)
    turned = [part.T for part in (cos_fine, sin_fine, cos_coarse, sin_coarse)]
    before()
    tiles = length // LANES
    for at in range(tiles):
        tile = cos_coarse[:, at : at + 1] * cos_fine - sin_coarse[:, at : at + 1] * sin_fine
        hi, lo = split_hi_lo(tile)
        a, col = divmod(at * LANES, width)
        bw[a, :bands, col : col + LANES] = hi
        bw[a, bands:, col : col + LANES] = lo
        tile = turned[2][at : at + 1] * turned[0] - turned[3][at : at + 1] * turned[1]
        hi, lo = split_hi_lo(tile)
        bt[at * LANES : (at + 1) * LANES, :bands] = hi
        bt[at * LANES : (at + 1) * LANES, bands:] = lo
        beside(at, tiles)


CORE, SIDES, DIAGONAL = 1, (2, 4), 6
ARRIVALS = ((0, CORE), (DIAGONAL, DIAGONAL + CORE), tuple(k + CORE for k in SIDES), SIDES)
PLACE = {k: i for i, k in enumerate(sum(ARRIVALS, ()))}
LAST_STEPS = 4


def kernel(
    n, reps, band_hbm, x_hbm, og_hbm, w_hbm, mom_hbm, left, nw, val,
    band, x, oc, og, w, mom, bw, bt, perm, xa, zc, grad, upd, even, odd, pin, vout, vin, hout, hin,
    cl, cpo, cpi, zo, zi, cx, sg,
    load_sem, send_sem, x_recv, og_recv, p_recv, v_recv, c_recv, side_entered, rep_round, all_entered,
):
    me, rep = lax.axis_index("fsdp"), lax.axis_index("rep")
    tokens, depth = x.shape
    own_rows, width = w.shape
    slabs, bands = bw.shape[0], bw.shape[1] // 2
    groups = mom.shape[0]
    half_tokens = tokens // 2
    scaling = 1.0 / math.sqrt(depth)
    bits = n.bit_length() - 1

    def peer(k):
        return sum((((me // 2**b) % 2 + (k >> b) % 2) % 2) * 2**b for b in range(bits))

    def columns(which):
        return pl.ds(pl.multiple_of(which * own_rows, LANES), own_rows)

    def to_peer(k, src, dst, send, recv):
        return pltpu.make_async_remote_copy(
            src_ref=src, dst_ref=dst, send_sem=send, recv_sem=recv,
            device_id={"fsdp": peer(k)}, device_id_type=pl.DeviceIdType.MESH,
        )

    def to_rep(d, src, dst, send, recv):
        return pltpu.make_async_remote_copy(
            src_ref=src, dst_ref=dst, send_sem=send, recv_sem=recv,
            device_id={"rep": lax.rem(rep + d, reps)}, device_id_type=pl.DeviceIdType.MESH,
        )

    def wait_bytes(like, sem):
        pltpu.make_async_copy(like, like, sem).wait()

    def wait_total(count, sem):
        like = bt.at[: count // (2 * bt.shape[1])]
        pltpu.make_async_copy(like, like, sem).wait()

    def signal_peer(sem, k):
        pl.semaphore_signal(sem, inc=1, device_id={"fsdp": peer(k)}, device_id_type=pl.DeviceIdType.MESH)

    first = me == 0

    def signal_next_reps(sem):
        for there, step in ((rep > 0, -1), (rep < reps - 1, 1)):

            @pl.when(first & there)
            def _():
                pl.semaphore_signal(
                    sem, inc=1, device_id={"rep": rep + step}, device_id_type=pl.DeviceIdType.MESH
                )

    next_reps = (rep > 0).astype(jnp.int32) + (rep < reps - 1).astype(jnp.int32)

    def pass_on(at):
        @pl.when(first)
        def _():
            pl.semaphore_wait(rep_round.at[at], next_reps)

        if at + 1 < reps - 1:
            signal_next_reps(rep_round.at[at + 1])
            return
        for k in range(1, n):

            @pl.when(first)
            def _():
                signal_peer(all_entered, k)

    barrier = pltpu.get_barrier_semaphore()
    near = [CORE] + [k + c for k in SIDES for c in (0, CORE)]
    signal_next_reps(barrier)
    for k in near:
        signal_peer(barrier, k)
    loads = [
        pltpu.make_async_copy(src, dst, load_sem.at[i])
        for i, src, dst in (
            (0, band_hbm, band),
            (1, x_hbm.at[0], x),
            (2, og_hbm.at[0], og.at[0]),
            (3, w_hbm, w),
            (3, mom_hbm.at[0], mom),
            (3, x_hbm.at[0, :, columns(me)], oc.at[0]),
        )
    ]
    for load in loads:
        load.start()
    pl.semaphore_wait(barrier, len(near) + jnp.where(first, next_reps, 0))

    signal_peer(side_entered, SIDES[0])
    block = 2 * tokens * width
    parts = [pl.ds(part * half_tokens, half_tokens) for part in range(2)]
    x_sem = {CORE: 0, DIAGONAL: 1, DIAGONAL + CORE: 2, **{k + CORE: 3 for k in SIDES}}
    og_sem = {CORE: 0, **{k: 1 for k in SIDES}, **{k + CORE: 2 for k in SIDES}, DIAGONAL + CORE: 4}
    og_copies = {
        k: to_peer(k, og_hbm.at[0], og.at[PLACE[k]], send_sem.at[0], og_recv.at[og_sem[k]]) for k in (*SIDES, CORE)
    }
    x_copies = {
        k: to_peer(
            k, x_hbm.at[0, :, columns(peer(k))], oc.at[PLACE[k]], send_sem.at[0], x_recv.at[x_sem[k]]
        )
        for k in x_sem
    }
    steps = [pl.ds(step * (tokens // LAST_STEPS), tokens // LAST_STEPS) for step in range(LAST_STEPS)]
    last_copies = [
        to_peer(
            k, x_hbm.at[0, steps[step], columns(peer(k))], oc.at[PLACE[k], steps[step]],
            send_sem.at[0], x_recv.at[4 + step],
        )
        for step in range(LAST_STEPS)
        for k in SIDES
    ]
    forward = {
        k: to_peer(
            CORE, og.at[PLACE[k]], og.at[PLACE[k + CORE]], send_sem.at[0], og_recv.at[og_sem[k + CORE]]
        )
        for k in (*SIDES, DIAGONAL)
    }
    relays = [
        to_peer(
            SIDES[side], og.at[PLACE[SIDES[1 - side]], parts[side]], og.at[PLACE[DIAGONAL], parts[side]],
            send_sem.at[0], og_recv.at[3],
        )
        for side in range(2)
    ]
    for copy in og_copies.values():
        copy.start()
    x_copies[CORE].start()

    span = slabs * LANES
    pieces = depth // span

    def before_tiles():
        row = lax.broadcasted_iota(jnp.int32, (span, LANES), 0)
        lane = lax.broadcasted_iota(jnp.int32, (span, LANES), 1)
        for a in range(slabs):
            perm[:, a * LANES : (a + 1) * LANES] = (row == slabs * lane + a).astype(F32).astype(BF16)
        pl.semaphore_wait(side_entered, 1)
        x_copies[DIAGONAL].start()
        x_copies[DIAGONAL + CORE].start()
        signal_next_reps(rep_round.at[0])

    def sort_tokens(at, steps):
        if (at + 1) * pieces % steps:
            return
        piece = (at + 1) * pieces // steps - 1
        sorted_piece = dot(x[:, piece * span : (piece + 1) * span], perm[...]).astype(BF16)
        for a in range(slabs):
            xa[a * tokens : (a + 1) * tokens, piece * LANES : (piece + 1) * LANES] = sorted_piece[
                :, a * LANES : (a + 1) * LANES
            ]

    loads[0].wait()
    loads[1].wait()
    fill_basis(band, bw, bt, before_tiles, sort_tokens)
    pass_on(0)

    loads[2].wait()
    for a in range(slabs):
        both = dot(og[0], bt[a * width : (a + 1) * width, :])
        hi, lo = split_hi_lo(both[:, :bands] + both[:, bands:])
        zc[a * tokens : (a + 1) * tokens, :bands] = hi
        zc[a * tokens : (a + 1) * tokens, bands:] = lo
    both = dot(xa[...], zc[...], ((0,), (0,)))
    cl[...] = (scaling * (both[:, :bands] + both[:, bands:])).reshape(n, groups, bands)
    core = lax.rem(me, 2)
    for c in range(n // 2):
        cpo[c] = cl[2 * c + 1 - core].astype(BF16)
    pair_copy = to_peer(CORE, cpo, cpi, send_sem.at[2], c_recv.at[0])
    pair_copy.start()

    pass_on(1)
    wait_bytes(og.at[:2], og_recv.at[1])
    for copy in relays:
        copy.start()
    for k in SIDES:
        forward[k].start()
        x_copies[k + CORE].start()
    def coefficients(slab_of):
        both = None
        for a in range(slabs):
            stacked = jnp.concatenate(split_hi_lo(slab_of(a)), 0)
            product = dot(stacked, bt[a * width : (a + 1) * width, :])
            both = product if both is None else both + product
        both = both[:, :bands] + both[:, bands:]
        return both[:groups] + both[groups:]

    wait_total(2 * own_rows * width + 4 * groups * slabs * width + 2 * tokens * own_rows, load_sem.at[3])
    from_momentum = coefficients(lambda a: MOMENTUM_DECAY * mom[:, a * width : (a + 1) * width])
    cl[me] += from_momentum
    for at in range(2, reps - 1):
        pass_on(at)
    pair_copy.wait_recv()
    for c in range(n // 2):
        cl[2 * c + core] += cpi[c].astype(F32)
        zo[c] = cl[2 * c + core].astype(BF16)

    @pl.when(jnp.logical_not(first))
    def _():
        pl.semaphore_wait(all_entered, 1)

    for d in range(1, reps):
        to_rep(d, zo.at[lax.rem(rep + d, reps)], zi.at[rep], send_sem.at[2], c_recv.at[1]).start()

    tiles = range(width // LANES)

    def to_partner(k, which):
        copy = to_peer(CORE, odd.at[k // 2], pin.at[k // 2], send_sem.at[1], p_recv.at[which])
        copy.start()
        return copy

    def add_gradient(pair):
        at = slice(2 * pair, 2 * pair + 2)
        product = dot(
            oc[at].reshape(2 * tokens, own_rows), og[at].reshape(2 * tokens, width), ((0,), (0,))
        )
        for t in tiles:
            cut = product[:, t * LANES : (t + 1) * LANES]
            grad[t] = cut if pair == 0 else grad[t] + cut

    x_copies[CORE].wait_recv()
    both = dot(oc[0:2].reshape(2 * tokens, own_rows), w[...])
    even[0] = both[:tokens]
    odd[0] = both[tokens:].astype(BF16)
    from_core = to_partner(CORE, 0)
    og_copies[CORE].wait_recv()
    add_gradient(0)
    x_copies[DIAGONAL].wait_recv()
    even[DIAGONAL // 2] = dot(oc[PLACE[DIAGONAL]], w[...])
    x_copies[DIAGONAL + CORE].wait_recv()
    odd[DIAGONAL // 2] = dot(oc[PLACE[DIAGONAL + CORE]], w[...]).astype(BF16)
    from_diagonal = to_partner(DIAGONAL + CORE, 1)
    wait_bytes(zi.at[: reps - 1], c_recv.at[1])
    plane_sum = cl[2 * rep + core]
    for d in range(1, reps):
        plane_sum = plane_sum + zi[lax.rem(rep + d, reps)].astype(F32)
    cx[0] = plane_sum.astype(BF16)
    for k in (*SIDES, DIAGONAL):
        to_peer(k, cx.at[0], cx.at[k // 2], send_sem.at[2], c_recv.at[2]).start()
    from_diagonal.wait_recv()
    across = even[DIAGONAL // 2] + pin[DIAGONAL // 2].astype(F32)
    for side, k in enumerate(SIDES):
        hout[side] = across[side * half_tokens : (side + 1) * half_tokens].astype(BF16)
        to_peer(k, hout.at[side], hin.at[side], send_sem.at[1], v_recv.at[0]).start()
    for copy in last_copies:
        copy.start()
    wait_bytes(og.at[0], og_recv.at[3])
    forward[DIAGONAL].start()
    wait_bytes(oc.at[:2], x_recv.at[3])
    at = slice(PLACE[SIDES[0] + CORE], PLACE[SIDES[1] + CORE] + 1)
    both = dot(oc[at].reshape(2 * tokens, own_rows), w[...])
    for side, k in enumerate(SIDES):
        odd[k // 2] = both[side * tokens : (side + 1) * tokens].astype(BF16)
        to_partner(k + CORE, 2)
    wait_bytes(cx.at[1:], c_recv.at[2])
    total = plane_sum
    for h in range(1, n // 2):
        total = total + cx[h].astype(F32)
    mine = 2 * rep + core
    sg[mine] = (total / reps).astype(BF16)
    for d in range(1, reps):
        to_rep(d, sg.at[mine], sg.at[mine], send_sem.at[2], c_recv.at[3]).start()
    to_peer(CORE, sg.at[mine], sg.at[mine], send_sem.at[2], c_recv.at[4]).start()
    forward[DIAGONAL].wait_recv()
    add_gradient(1)
    wait_bytes(og.at[:2], og_recv.at[2])
    add_gradient(2)

    wait_bytes(pin.at[:2], p_recv.at[2])
    wait_bytes(hin, v_recv.at[0])
    for step in range(LAST_STEPS):
        rows = tokens // LAST_STEPS
        cut = slice(step * rows, (step + 1) * rows)
        part, within = divmod(step * rows, half_tokens)
        wait_bytes(oc.at[:2, steps[0]], x_recv.at[4 + step])
        for side, k in enumerate(SIDES):
            ours = dot(oc[PLACE[k], cut], w[...]) + pin[k // 2, cut].astype(F32)
            if part != side:
                ours = ours + hin[part, within : within + rows].astype(F32)
            vout[side, cut] = ours.astype(BF16)
            to_peer(k, vout.at[side, steps[step]], vin.at[side, steps[step]], send_sem.at[1], v_recv.at[1]).start()
    add_gradient(3)

    def gradient_slab(a):
        rows = [grad[t, pl.ds(a, groups, stride=slabs), :] for t in tiles]
        return scaling * jnp.concatenate(rows, 1)

    def keep_moment(a):
        part = gradient_slab(a)
        cut = slice(a * width, (a + 1) * width)
        mom[:, cut] = MOMENTUM_DECAY * mom[:, cut] + part
        return part

    kept = doubled(from_momentum + coefficients(keep_moment))
    wait_bytes(sg.at[: reps - 1], c_recv.at[3])
    for d in range(1, reps):
        slot = 2 * lax.rem(rep + d, reps) + core
        to_peer(CORE, sg.at[slot], sg.at[slot], send_sem.at[2], c_recv.at[4]).start()
    from_core.wait_recv()
    for a in range(slabs):
        cut = slice(a * width, (a + 1) * width)
        both = dot(kept, bw[a])
        left[0, :, cut] = mom[:, cut] - (both[:groups] + both[groups:])
    agreed = jnp.concatenate([sg[me]] * 2, 1)
    for a in range(slabs):
        product = dot(agreed, bw[a])
        for t in tiles:
            upd[t, pl.ds(a, groups, stride=slabs), :] = product[:, t * LANES : (t + 1) * LANES]
    for t in tiles:
        cut = slice(t * LANES, (t + 1) * LANES)
        nw[:, cut] = rebuild_rows(w[:, cut], upd[t])
    wait_bytes(sg.at[: n // 2], c_recv.at[4])
    mixed = dot(xa[...], sg[...].reshape(n * groups, bands)).astype(BF16)
    mixed = [mixed[a * tokens : (a + 1) * tokens] for a in range(slabs) for _ in range(2)]
    change = dot(jnp.concatenate(mixed, 1), bw[...].reshape(2 * slabs * bands, width))
    base = even[0] + pin[0].astype(F32) - LEARNING_RATE * change
    wait_bytes(vin, v_recv.at[1])
    for side in range(2):
        base = base + vin[side].astype(F32)
    val[0] = (base * scaling).astype(BF16)

    wait_total(14 * block, send_sem.at[0])
    wait_total(7 * block, send_sem.at[1])
    wait_total((3 * (n // 2) - 1 + 2 * (reps - 1)) * 2 * groups * bands, send_sem.at[2])


def store_kernel(left, nw, val, left_hbm, nw_hbm, val_hbm, sems):
    copies = [
        pltpu.make_async_copy(src, dst, sems.at[i])
        for i, (src, dst) in enumerate(((left, left_hbm), (nw, nw_hbm), (val, val_hbm)))
    ]
    for copy in copies:
        copy.start()
    for copy in copies:
        copy.wait()


def fused_shards(n, reps, inputs, out_grad, weight, momentum, band_index):
    tokens, depth = inputs.shape[1:]
    own_rows, width = weight.shape
    groups, group_len = momentum.shape[1:]
    slabs, bands = group_len // width, band_index.shape[0]
    half = n // 2
    dma, regular = pltpu.SemaphoreType.DMA, pltpu.SemaphoreType.REGULAR
    span = slabs * LANES
    anywhere = pl.BlockSpec(memory_space=pl.ANY)
    held = pl.pallas_call(
        functools.partial(kernel, n, reps),
        out_shape=(
            pltpu.VMEM(momentum.shape, F32),
            pltpu.VMEM(weight.shape, BF16),
            pltpu.VMEM(out_grad.shape, BF16),
        ),
        in_specs=[anywhere] * 5,
        out_specs=(pl.BlockSpec(memory_space=pltpu.VMEM),) * 3,
        scratch_shapes=[
            pltpu.VMEM((1, bands), jnp.int32),
            pltpu.VMEM((tokens, depth), BF16),
            pltpu.VMEM((n, tokens, own_rows), BF16),
            pltpu.VMEM((n, tokens, width), BF16),
            pltpu.VMEM((own_rows, width), BF16),
            pltpu.VMEM((groups, group_len), F32),
            pltpu.VMEM((slabs, 2 * bands, width), BF16),
            pltpu.VMEM((group_len, 2 * bands), BF16),
            pltpu.VMEM((span, span), BF16),
            pltpu.VMEM((slabs * tokens, depth // slabs), BF16),
            pltpu.VMEM((slabs * tokens, 2 * bands), BF16),
            pltpu.VMEM((width // LANES, own_rows, LANES), F32),
            pltpu.VMEM((width // LANES, own_rows, LANES), F32),
            pltpu.VMEM((half, tokens, width), F32),
            pltpu.VMEM((half, tokens, width), BF16),
            pltpu.VMEM((half, tokens, width), BF16),
            pltpu.VMEM((2, tokens, width), BF16),
            pltpu.VMEM((2, tokens, width), BF16),
            pltpu.VMEM((2, tokens // 2, width), BF16),
            pltpu.VMEM((2, tokens // 2, width), BF16),
            pltpu.VMEM((n, groups, bands), F32),
            pltpu.VMEM((half, groups, bands), BF16),
            pltpu.VMEM((half, groups, bands), BF16),
            pltpu.VMEM((half, groups, bands), BF16),
            pltpu.VMEM((half, groups, bands), BF16),
            pltpu.VMEM((half, groups, bands), BF16),
            pltpu.VMEM((n, groups, bands), BF16),
            dma((4,)), dma((3,)), dma((4 + LAST_STEPS,)), dma((5,)), dma((3,)), dma((2,)), dma((5,)),
            regular, regular((reps - 1,)), regular,
        ],
        compiler_params=pltpu.CompilerParams(collective_id=0, has_side_effects=True),
    )(band_index.reshape(1, -1), inputs, out_grad, weight, momentum)
    return pl.pallas_call(
        store_kernel,
        out_shape=tuple(jax.ShapeDtypeStruct(a.shape, a.dtype) for a in held),
        in_specs=[anywhere] * 3,
        out_specs=(anywhere,) * 3,
        scratch_shapes=[dma((3,))],
        compiler_params=pltpu.CompilerParams(vmem_limit_bytes=1 << 20),
    )(*held)


def fits_kernel(n, reps, inputs, weight, momentum, band_index):
    tokens, depth = inputs.shape[1:]
    own_rows, width = weight.shape
    groups, group_len = momentum.shape[1:]
    return (
        n == CORE + DIAGONAL + 1
        and reps == n // 2
        and group_len & (group_len - 1) == 0
        and tokens % (16 * LAST_STEPS) == 0
        and own_rows % LANES == 0
        and own_rows == width
        and width % LANES == 0
        and groups % 16 == 0
        and group_len % width == 0
        and group_len // LANES <= LANES
        and depth % (group_len // width * LANES) == 0
        and n * groups * (group_len // width) == depth
        and band_index.shape[0] % LANES == 0
    )


def program(n, reps, inputs, out_grad, weight, momentum, band_index):
    if fits_kernel(n, reps, inputs, weight, momentum, band_index):
        return fused_shards(n, reps, inputs, out_grad, weight, momentum, band_index)
    return shards(inputs, out_grad, weight, momentum, band_index)


def solution(mesh):
    placed = (
        P("rep", "fsdp", None),
        P("rep", "fsdp", None),
        P("fsdp", None),
        P("rep", "fsdp", None),
        P(),
    )
    return jax.shard_map(
        functools.partial(program, mesh.shape["fsdp"], mesh.shape["rep"]),
        mesh=mesh,
        in_specs=placed,
        out_specs=(P("rep", "fsdp", None), P("fsdp", None), P("rep", "fsdp", None)),
        check_vma=False,
    )
```

```python
import functools
import math

import jax
import jax.numpy as jnp
from jax import lax
from jax.experimental import pallas as pl
from jax.experimental.pallas import tpu as pltpu
from jax.sharding import PartitionSpec as P

MOMENTUM_DECAY = 0.9
LEARNING_RATE = 4.0


def dct_rows(band_index, length):
    positions = lax.iota(jnp.int32, length)
    phase_int = (2 * positions[None, :] + 1) * band_index[:, None] % (4 * length)
    angles = phase_int.astype(jnp.float32) * (math.pi / (2 * length))
    row_scale = jnp.where(band_index == 0, math.sqrt(1.0 / length), math.sqrt(2.0 / length)).astype(
        jnp.float32
    )
    return row_scale[:, None] * jnp.cos(angles)


def rebuild_rows(old_rows, update_rows):
    return (old_rows.astype(jnp.float32) - LEARNING_RATE * update_rows).astype(jnp.bfloat16)


def shards(inputs, out_grad, weight, momentum, band_index):
    tok_inputs = inputs[0]
    upstream = out_grad[0]
    own_rows = weight.shape[0]
    width_out = weight.shape[1]
    group_len = momentum.shape[2]
    scaling = 1.0 / math.sqrt(tok_inputs.shape[1])
    highest = lax.Precision.HIGHEST
    own_columns = lax.all_to_all(tok_inputs, "fsdp", split_axis=1, concat_axis=0, tiled=True)
    gradient = (
        lax.dot_general(
            own_columns,
            lax.all_gather(upstream, "fsdp", axis=0, tiled=True),
            (((0,), (0,)), ((), ())),
            preferred_element_type=jnp.float32,
        )
        * scaling
    )
    moment = MOMENTUM_DECAY * momentum[0] + gradient.reshape(-1, group_len)
    dct_basis = dct_rows(band_index, group_len)
    coeffs = jnp.dot(moment, dct_basis.T, precision=highest)
    leftover = (moment - jnp.dot(coeffs, dct_basis, precision=highest))[None]
    shared = lax.psum(coeffs, "rep") / lax.axis_size("rep")
    own_update = jnp.dot(shared, dct_basis, precision=highest).reshape(own_rows, width_out)
    new_weight = rebuild_rows(weight, own_update)
    running = jnp.dot(
        tok_inputs,
        lax.all_gather(new_weight, "fsdp", axis=0, tiled=True),
        preferred_element_type=jnp.float32,
    )
    values = (running * scaling).astype(jnp.bfloat16)[None]
    return (leftover, new_weight, values)


LANES = 128
F32, BF16 = jnp.float32, jnp.bfloat16


def split_hi_lo(x):
    hi = x.astype(BF16)
    return hi, (x - hi.astype(F32)).astype(BF16)


def dot(a, b, dims=((1,), (0,))):
    return lax.dot_general(a, b, (dims, ((), ())), preferred_element_type=F32)


def doubled(x):
    hi, lo = split_hi_lo(x)
    return jnp.concatenate([jnp.concatenate([part, part], 1) for part in (hi, lo)], 0)


def fill_basis(band_ref, bw, bt, before, beside):
    slabs, bands, width = bw.shape
    bands //= 2
    length = slabs * width
    period = 4 * length
    freq = jnp.broadcast_to(band_ref[...].astype(F32), (LANES, bands)).T.astype(jnp.int32)
    lane = lax.broadcasted_iota(jnp.int32, (bands, LANES), 1)
    row_scale = jnp.where(freq == 0, math.sqrt(1.0 / length), math.sqrt(2.0 / length)).astype(F32)

    def angle(steps):
        centred = ((steps * freq + period // 2) & (period - 1)) - period // 2
        return centred.astype(F32) * (math.pi / (2 * length))

    fine, coarse = angle(2 * lane + 1), angle(2 * LANES * lane)
    cos_fine, sin_fine = row_scale * jnp.cos(fine), row_scale * jnp.sin(fine)
    cos_coarse, sin_coarse = jnp.cos(coarse), jnp.sin(coarse)
    turned = [part.T for part in (cos_fine, sin_fine, cos_coarse, sin_coarse)]
    before()
    tiles = length // LANES
    for at in range(tiles):
        tile = cos_coarse[:, at : at + 1] * cos_fine - sin_coarse[:, at : at + 1] * sin_fine
        hi, lo = split_hi_lo(tile)
        a, col = divmod(at * LANES, width)
        bw[a, :bands, col : col + LANES] = hi
        bw[a, bands:, col : col + LANES] = lo
        tile = turned[2][at : at + 1] * turned[0] - turned[3][at : at + 1] * turned[1]
        hi, lo = split_hi_lo(tile)
        bt[at * LANES : (at + 1) * LANES, :bands] = hi
        bt[at * LANES : (at + 1) * LANES, bands:] = lo
        beside(at, tiles)


CORE, SIDES, DIAGONAL = 1, (2, 4), 6
ARRIVALS = ((0, CORE), (DIAGONAL, DIAGONAL + CORE), tuple(k + CORE for k in SIDES), SIDES)
PLACE = {k: i for i, k in enumerate(sum(ARRIVALS, ()))}
LAST_STEPS = 4


def kernel(
    n, reps, band_hbm, x_hbm, og_hbm, w_hbm, mom_hbm, left, nw, val,
    band, x, oc, og, w, mom, bw, bt, perm, xa, zc, grad, upd, even, odd, pin, vout, vin, hout, hin,
    cl, cpo, cpi, zo, zi, cx, sg,
    load_sem, send_sem, x_recv, og_recv, p_recv, v_recv, c_recv, side_entered, next_entered, rep_round,
):
    me, rep = lax.axis_index("fsdp"), lax.axis_index("rep")
    tokens, depth = x.shape
    own_rows, width = w.shape
    slabs, bands = bw.shape[0], bw.shape[1] // 2
    groups = mom.shape[0]
    half_tokens = tokens // 2
    scaling = 1.0 / math.sqrt(depth)
    bits = n.bit_length() - 1

    def peer(k):
        return sum((((me // 2**b) % 2 + (k >> b) % 2) % 2) * 2**b for b in range(bits))

    def columns(which):
        return pl.ds(pl.multiple_of(which * own_rows, LANES), own_rows)

    def to_peer(k, src, dst, send, recv):
        return pltpu.make_async_remote_copy(
            src_ref=src, dst_ref=dst, send_sem=send, recv_sem=recv,
            device_id={"fsdp": peer(k)}, device_id_type=pl.DeviceIdType.MESH,
        )

    def to_rep(d, src, dst, send, recv):
        return pltpu.make_async_remote_copy(
            src_ref=src, dst_ref=dst, send_sem=send, recv_sem=recv,
            device_id={"rep": lax.rem(rep + d, reps)}, device_id_type=pl.DeviceIdType.MESH,
        )

    def wait_bytes(like, sem):
        pltpu.make_async_copy(like, like, sem).wait()

    def wait_total(count, sem):
        like = bt.at[: count // (2 * bt.shape[1])]
        pltpu.make_async_copy(like, like, sem).wait()

    def signal_peer(sem, k):
        pl.semaphore_signal(sem, inc=1, device_id={"fsdp": peer(k)}, device_id_type=pl.DeviceIdType.MESH)

    def signal_rep(sem, step):
        @pl.when(rep > 0 if step < 0 else rep < reps - 1)
        def _():
            pl.semaphore_signal(sem, inc=1, device_id={"rep": rep + step}, device_id_type=pl.DeviceIdType.MESH)

    below, above = (rep > 0).astype(jnp.int32), (rep < reps - 1).astype(jnp.int32)

    def hear_reps(at):
        if at == 0:

            @pl.when(rep < reps - 1)
            def _():
                pl.semaphore_wait(next_entered, 1)

        else:
            pl.semaphore_wait(rep_round.at[at - 1], below + above)
        if at < reps - 2:
            for step in (-1, 1):
                signal_rep(rep_round.at[at], step)

    barrier = pltpu.get_barrier_semaphore()
    core = lax.rem(me, 2)
    near = [CORE] + [k + c for k in SIDES for c in (0, CORE)]
    signal_rep(barrier, 1)
    for k in near:
        signal_peer(barrier, k)
    loads = [
        pltpu.make_async_copy(src, dst, load_sem.at[i])
        for i, src, dst in (
            (0, band_hbm, band),
            (1, x_hbm.at[0], x),
            (2, og_hbm.at[0], og.at[0]),
            (3, w_hbm, w),
            (3, mom_hbm.at[0], mom),
            (3, x_hbm.at[0, :, columns(me)], oc.at[0]),
        )
    ]
    for load in loads:
        load.start()
    pl.semaphore_wait(barrier, len(near) + below)

    signal_peer(side_entered, SIDES[0])
    signal_rep(next_entered, -1)
    block = 2 * tokens * width
    parts = [pl.ds(part * half_tokens, half_tokens) for part in range(2)]
    x_sem = {CORE: 0, DIAGONAL: 1, DIAGONAL + CORE: 2, **{k + CORE: 3 for k in SIDES}}
    og_sem = {CORE: 0, **{k: 1 for k in SIDES}, **{k + CORE: 2 for k in SIDES}, DIAGONAL + CORE: 4}
    og_copies = {
        k: to_peer(k, og_hbm.at[0], og.at[PLACE[k]], send_sem.at[0], og_recv.at[og_sem[k]]) for k in (*SIDES, CORE)
    }
    x_copies = {
        k: to_peer(
            k, x_hbm.at[0, :, columns(peer(k))], oc.at[PLACE[k]], send_sem.at[0], x_recv.at[x_sem[k]]
        )
        for k in x_sem
    }
    steps = [pl.ds(step * (tokens // LAST_STEPS), tokens // LAST_STEPS) for step in range(LAST_STEPS)]
    last_copies = [
        to_peer(
            k, x_hbm.at[0, steps[step], columns(peer(k))], oc.at[PLACE[k], steps[step]],
            send_sem.at[0], x_recv.at[4 + step],
        )
        for step in range(LAST_STEPS)
        for k in SIDES
    ]
    forward = {
        k: to_peer(
            CORE, og.at[PLACE[k]], og.at[PLACE[k + CORE]], send_sem.at[0], og_recv.at[og_sem[k + CORE]]
        )
        for k in (*SIDES, DIAGONAL)
    }
    relays = [
        to_peer(
            SIDES[side] + c, og.at[PLACE[SIDES[1 - side] + c], parts[side]], og.at[PLACE[DIAGONAL], parts[side]],
            send_sem.at[0], og_recv.at[3],
        )
        for side in range(2)
        for c in (0, CORE)
    ]
    for copy in og_copies.values():
        copy.start()
    x_copies[CORE].start()

    span = slabs * LANES
    pieces = depth // span

    def before_tiles():
        row = lax.broadcasted_iota(jnp.int32, (span, LANES), 0)
        lane = lax.broadcasted_iota(jnp.int32, (span, LANES), 1)
        for a in range(slabs):
            perm[:, a * LANES : (a + 1) * LANES] = (row == slabs * lane + a).astype(F32).astype(BF16)
        pl.semaphore_wait(side_entered, 1)
        x_copies[DIAGONAL].start()
        x_copies[DIAGONAL + CORE].start()

    def sort_tokens(at, steps):
        if (at + 1) * pieces % steps:
            return
        piece = (at + 1) * pieces // steps - 1
        sorted_piece = dot(x[:, piece * span : (piece + 1) * span], perm[...]).astype(BF16)
        for a in range(slabs):
            xa[a * tokens : (a + 1) * tokens, piece * LANES : (piece + 1) * LANES] = sorted_piece[
                :, a * LANES : (a + 1) * LANES
            ]

    loads[0].wait()
    loads[1].wait()
    fill_basis(band, bw, bt, before_tiles, sort_tokens)
    hear_reps(0)

    loads[2].wait()
    for a in range(slabs):
        both = dot(og[0], bt[a * width : (a + 1) * width, :])
        hi, lo = split_hi_lo(both[:, :bands] + both[:, bands:])
        zc[a * tokens : (a + 1) * tokens, :bands] = hi
        zc[a * tokens : (a + 1) * tokens, bands:] = lo
    both = dot(xa[...], zc[...], ((0,), (0,)))
    cl[...] = (scaling * (both[:, :bands] + both[:, bands:])).reshape(n, groups, bands)
    for c in range(n // 2):
        cpo[c] = cl[2 * c + 1 - core].astype(BF16)
    pair_copy = to_peer(CORE, cpo, cpi, send_sem.at[2], c_recv.at[0])
    pair_copy.start()

    hear_reps(1)
    wait_bytes(og.at[:2], og_recv.at[1])
    for k in SIDES:
        forward[k].start()
        x_copies[k + CORE].start()
    def coefficients(slab_of):
        both = None
        for a in range(slabs):
            stacked = jnp.concatenate(split_hi_lo(slab_of(a)), 0)
            product = dot(stacked, bt[a * width : (a + 1) * width, :])
            both = product if both is None else both + product
        both = both[:, :bands] + both[:, bands:]
        return both[:groups] + both[groups:]

    wait_total(2 * own_rows * width + 4 * groups * slabs * width + 2 * tokens * own_rows, load_sem.at[3])
    from_momentum = coefficients(lambda a: MOMENTUM_DECAY * mom[:, a * width : (a + 1) * width])
    cl[me] += from_momentum
    for at in range(2, reps - 1):
        hear_reps(at)
    pair_copy.wait_recv()
    for c in range(n // 2):
        cl[2 * c + core] += cpi[c].astype(F32)
        zo[c] = cl[2 * c + core].astype(BF16)
    for d in range(1, reps):
        to_rep(d, zo.at[lax.rem(rep + d, reps)], zi.at[rep], send_sem.at[2], c_recv.at[1]).start()

    tiles = range(width // LANES)

    def to_partner(k, which):
        copy = to_peer(CORE, odd.at[k // 2], pin.at[k // 2], send_sem.at[1], p_recv.at[which])
        copy.start()
        return copy

    def add_gradient(pair):
        at = slice(2 * pair, 2 * pair + 2)
        product = dot(
            oc[at].reshape(2 * tokens, own_rows), og[at].reshape(2 * tokens, width), ((0,), (0,))
        )
        for t in tiles:
            cut = product[:, t * LANES : (t + 1) * LANES]
            grad[t] = cut if pair == 0 else grad[t] + cut

    x_copies[CORE].wait_recv()
    both = dot(oc[0:2].reshape(2 * tokens, own_rows), w[...])
    even[0] = both[:tokens]
    odd[0] = both[tokens:].astype(BF16)
    from_core = to_partner(CORE, 0)
    og_copies[CORE].wait_recv()
    add_gradient(0)
    wait_bytes(og.at[:2], og_recv.at[2])

    @pl.when(core == 1)
    def _():
        for copy in relays:
            copy.start()

    wait_bytes(zi.at[: reps - 1], c_recv.at[1])
    plane_sum = cl[2 * rep + core]
    for d in range(1, reps):
        plane_sum = plane_sum + zi[lax.rem(rep + d, reps)].astype(F32)
    cx[0] = plane_sum.astype(BF16)
    for k in (*SIDES, DIAGONAL):
        to_peer(k, cx.at[0], cx.at[k // 2], send_sem.at[2], c_recv.at[2]).start()
    x_copies[DIAGONAL].wait_recv()
    even[DIAGONAL // 2] = dot(oc[PLACE[DIAGONAL]], w[...])
    x_copies[DIAGONAL + CORE].wait_recv()
    odd[DIAGONAL // 2] = dot(oc[PLACE[DIAGONAL + CORE]], w[...]).astype(BF16)
    from_diagonal = to_partner(DIAGONAL + CORE, 1)
    from_diagonal.wait_recv()
    across = even[DIAGONAL // 2] + pin[DIAGONAL // 2].astype(F32)
    for side, k in enumerate(SIDES):
        hout[side] = across[side * half_tokens : (side + 1) * half_tokens].astype(BF16)
        to_peer(k, hout.at[side], hin.at[side], send_sem.at[1], v_recv.at[0]).start()
    for copy in last_copies:
        copy.start()
    wait_bytes(oc.at[:2], x_recv.at[3])
    at = slice(PLACE[SIDES[0] + CORE], PLACE[SIDES[1] + CORE] + 1)
    both = dot(oc[at].reshape(2 * tokens, own_rows), w[...])
    for side, k in enumerate(SIDES):
        odd[k // 2] = both[side * tokens : (side + 1) * tokens].astype(BF16)
        to_partner(k + CORE, 2)
    wait_bytes(cx.at[1:], c_recv.at[2])
    total = plane_sum
    for h in range(1, n // 2):
        total = total + cx[h].astype(F32)
    mine = 2 * rep + core
    sg[mine] = (total / reps).astype(BF16)
    for d in range(1, reps):
        to_rep(d, sg.at[mine], sg.at[mine], send_sem.at[2], c_recv.at[3]).start()
    to_peer(CORE, sg.at[mine], sg.at[mine], send_sem.at[2], c_recv.at[4]).start()
    wait_bytes(og.at[0], og_recv.at[3])
    forward[DIAGONAL].start()
    add_gradient(2)
    forward[DIAGONAL].wait_recv()
    add_gradient(1)

    wait_bytes(pin.at[:2], p_recv.at[2])
    wait_bytes(hin, v_recv.at[0])
    for step in range(LAST_STEPS):
        rows = tokens // LAST_STEPS
        cut = slice(step * rows, (step + 1) * rows)
        part, within = divmod(step * rows, half_tokens)
        wait_bytes(oc.at[:2, steps[0]], x_recv.at[4 + step])
        for side, k in enumerate(SIDES):
            ours = dot(oc[PLACE[k], cut], w[...]) + pin[k // 2, cut].astype(F32)
            if part != side:
                ours = ours + hin[part, within : within + rows].astype(F32)
            vout[side, cut] = ours.astype(BF16)
            to_peer(k, vout.at[side, steps[step]], vin.at[side, steps[step]], send_sem.at[1], v_recv.at[1]).start()
    add_gradient(3)

    def gradient_slab(a):
        rows = [grad[t, pl.ds(a, groups, stride=slabs), :] for t in tiles]
        return scaling * jnp.concatenate(rows, 1)

    def keep_moment(a):
        part = gradient_slab(a)
        cut = slice(a * width, (a + 1) * width)
        mom[:, cut] = MOMENTUM_DECAY * mom[:, cut] + part
        return part

    kept = doubled(from_momentum + coefficients(keep_moment))
    wait_bytes(sg.at[: reps - 1], c_recv.at[3])
    for d in range(1, reps):
        slot = 2 * lax.rem(rep + d, reps) + core
        to_peer(CORE, sg.at[slot], sg.at[slot], send_sem.at[2], c_recv.at[4]).start()
    from_core.wait_recv()
    for a in range(slabs):
        cut = slice(a * width, (a + 1) * width)
        both = dot(kept, bw[a])
        left[0, :, cut] = mom[:, cut] - (both[:groups] + both[groups:])
    agreed = jnp.concatenate([sg[me]] * 2, 1)
    for a in range(slabs):
        product = dot(agreed, bw[a])
        for t in tiles:
            upd[t, pl.ds(a, groups, stride=slabs), :] = product[:, t * LANES : (t + 1) * LANES]
    for t in tiles:
        cut = slice(t * LANES, (t + 1) * LANES)
        nw[:, cut] = rebuild_rows(w[:, cut], upd[t])
    wait_bytes(sg.at[: n // 2], c_recv.at[4])
    mixed = dot(xa[...], sg[...].reshape(n * groups, bands)).astype(BF16)
    mixed = [mixed[a * tokens : (a + 1) * tokens] for a in range(slabs) for _ in range(2)]
    change = dot(jnp.concatenate(mixed, 1), bw[...].reshape(2 * slabs * bands, width))
    base = even[0] + pin[0].astype(F32) - LEARNING_RATE * change
    wait_bytes(vin, v_recv.at[1])
    for side in range(2):
        base = base + vin[side].astype(F32)
    val[0] = (base * scaling).astype(BF16)

    for value, blocks in ((0, 13), (1, 15)):

        @pl.when(core == value)
        def _():
            wait_total(blocks * block, send_sem.at[0])

    wait_total(7 * block, send_sem.at[1])
    wait_total((3 * (n // 2) - 1 + 2 * (reps - 1)) * 2 * groups * bands, send_sem.at[2])


def store_kernel(left, nw, val, left_hbm, nw_hbm, val_hbm, sems):
    copies = [
        pltpu.make_async_copy(src, dst, sems.at[i])
        for i, (src, dst) in enumerate(((left, left_hbm), (nw, nw_hbm), (val, val_hbm)))
    ]
    for copy in copies:
        copy.start()
    for copy in copies:
        copy.wait()


def fused_shards(n, reps, inputs, out_grad, weight, momentum, band_index):
    tokens, depth = inputs.shape[1:]
    own_rows, width = weight.shape
    groups, group_len = momentum.shape[1:]
    slabs, bands = group_len // width, band_index.shape[0]
    half = n // 2
    dma, regular = pltpu.SemaphoreType.DMA, pltpu.SemaphoreType.REGULAR
    span = slabs * LANES
    anywhere = pl.BlockSpec(memory_space=pl.ANY)
    held = pl.pallas_call(
        functools.partial(kernel, n, reps),
        out_shape=(
            pltpu.VMEM(momentum.shape, F32),
            pltpu.VMEM(weight.shape, BF16),
            pltpu.VMEM(out_grad.shape, BF16),
        ),
        in_specs=[anywhere] * 5,
        out_specs=(pl.BlockSpec(memory_space=pltpu.VMEM),) * 3,
        scratch_shapes=[
            pltpu.VMEM((1, bands), jnp.int32),
            pltpu.VMEM((tokens, depth), BF16),
            pltpu.VMEM((n, tokens, own_rows), BF16),
            pltpu.VMEM((n, tokens, width), BF16),
            pltpu.VMEM((own_rows, width), BF16),
            pltpu.VMEM((groups, group_len), F32),
            pltpu.VMEM((slabs, 2 * bands, width), BF16),
            pltpu.VMEM((group_len, 2 * bands), BF16),
            pltpu.VMEM((span, span), BF16),
            pltpu.VMEM((slabs * tokens, depth // slabs), BF16),
            pltpu.VMEM((slabs * tokens, 2 * bands), BF16),
            pltpu.VMEM((width // LANES, own_rows, LANES), F32),
            pltpu.VMEM((width // LANES, own_rows, LANES), F32),
            pltpu.VMEM((half, tokens, width), F32),
            pltpu.VMEM((half, tokens, width), BF16),
            pltpu.VMEM((half, tokens, width), BF16),
            pltpu.VMEM((2, tokens, width), BF16),
            pltpu.VMEM((2, tokens, width), BF16),
            pltpu.VMEM((2, tokens // 2, width), BF16),
            pltpu.VMEM((2, tokens // 2, width), BF16),
            pltpu.VMEM((n, groups, bands), F32),
            pltpu.VMEM((half, groups, bands), BF16),
            pltpu.VMEM((half, groups, bands), BF16),
            pltpu.VMEM((half, groups, bands), BF16),
            pltpu.VMEM((half, groups, bands), BF16),
            pltpu.VMEM((half, groups, bands), BF16),
            pltpu.VMEM((n, groups, bands), BF16),
            dma((4,)), dma((3,)), dma((4 + LAST_STEPS,)), dma((5,)), dma((3,)), dma((2,)), dma((5,)),
            regular, regular, regular((reps - 2,)),
        ],
        compiler_params=pltpu.CompilerParams(collective_id=0, has_side_effects=True),
    )(band_index.reshape(1, -1), inputs, out_grad, weight, momentum)
    return pl.pallas_call(
        store_kernel,
        out_shape=tuple(jax.ShapeDtypeStruct(a.shape, a.dtype) for a in held),
        in_specs=[anywhere] * 3,
        out_specs=(anywhere,) * 3,
        scratch_shapes=[dma((3,))],
        compiler_params=pltpu.CompilerParams(vmem_limit_bytes=1 << 20),
    )(*held)


def fits_kernel(n, reps, inputs, weight, momentum, band_index):
    tokens, depth = inputs.shape[1:]
    own_rows, width = weight.shape
    groups, group_len = momentum.shape[1:]
    return (
        n == CORE + DIAGONAL + 1
        and reps == n // 2 > 2
        and group_len & (group_len - 1) == 0
        and tokens % (16 * LAST_STEPS) == 0
        and own_rows % LANES == 0
        and own_rows == width
        and width % LANES == 0
        and groups % 16 == 0
        and group_len % width == 0
        and group_len // LANES <= LANES
        and depth % (group_len // width * LANES) == 0
        and n * groups * (group_len // width) == depth
        and band_index.shape[0] % LANES == 0
    )


def program(n, reps, inputs, out_grad, weight, momentum, band_index):
    if fits_kernel(n, reps, inputs, weight, momentum, band_index):
        return fused_shards(n, reps, inputs, out_grad, weight, momentum, band_index)
    return shards(inputs, out_grad, weight, momentum, band_index)


def solution(mesh):
    placed = (
        P("rep", "fsdp", None),
        P("rep", "fsdp", None),
        P("fsdp", None),
        P("rep", "fsdp", None),
        P(),
    )
    return jax.shard_map(
        functools.partial(program, mesh.shape["fsdp"], mesh.shape["rep"]),
        mesh=mesh,
        in_specs=placed,
        out_specs=(P("rep", "fsdp", None), P("fsdp", None), P("rep", "fsdp", None)),
        check_vma=False,
    )
```
